128 devices in a mesh: seq: 64 (over z, y, x), head: 2 (over core).
Axes of the slice: x: 4, y: 4, z: 4, core: 2. Of those that a mesh axis runs over, the one named last changes fastest.
Arguments:
- query: bfloat16 [8192, 4096], P('seq', 'head'), may hold values from -6 to 6
- keys: bfloat16 [8192, 2, 4096], P('seq', None, 'head'), may hold values from -8 to 8
- values: bfloat16 [8192, 2, 4096], P('seq', None, 'head'), may hold values from -6 to 6
- beta: float32 [2, 32, 8192], P(None, 'head', 'seq'), may hold values from 0.001 to 1
- gate_log: float32 [32, 8192], P('head', 'seq'), may hold values from -0.7 to 0
- house_count: int32 [8192], P('seq'), may hold values from 1 to 2
- out_gate: bfloat16 [8192, 4096], P('seq', 'head'), may hold values from -6 to 6
- norm_gain: float32 [128], replicated, may hold values from 0.1 to 1.9
- out_weight: bfloat16 [4096, 4096], P(None, 'head'), may hold values from -0.09375 to 0.09375
Outputs:
- mixed: bfloat16 [8192, 4096], P('seq', 'head')
The draws below stay inside these ranges and needn't reach their ends.
All inputs are finite; a program needn't handle non-finite values.
Results may differ from the reference program's by a relative error of at most 0.0049.
Values may be sent and summed in bfloat16 or wider, within the bound.
No kernel may reach another device: no remote copies, remote signals or barrier semaphores. Data moves between devices by JAX's collectives and lax.ppermute only.
A program may use at most 320 MiB of HBM per device.

```python
import math
import jax
import jax.numpy as jnp
from jax import lax

H = 32
DK = 128
DV = 128
D = 4096
NH = 2
DOCUMENT_TOKENS = 8192


def head_kinds(key):
    order = jax.random.permutation(jax.random.fold_in(key, 7), H)
    fast_count = H // 2
    return (order < fast_count)[:, None]


def draw_gate_log(key, part):
    fast_key, slow_key, rough_key, position_key, retained_key = jax.random.split(jax.random.fold_in(key, 3), 5)
    is_fast = head_kinds(key)
    rate_fast = math.log(10.0) / jax.random.uniform(fast_key, (H, 1), minval=30.0, maxval=50.0)
    rate_slow = jax.random.uniform(slow_key, (H, 1), minval=0.1, maxval=0.4) / DOCUMENT_TOKENS
    head_decay_rates = jnp.where(is_fast, rate_fast, rate_slow)
    noise_level = jnp.exp(jax.random.uniform(rough_key, (H, DOCUMENT_TOKENS), minval=-math.log(2.0), maxval=math.log(2.0)))
    cluster_positions = jax.random.randint(position_key, (3, 1), 0, DOCUMENT_TOKENS)
    cluster_keep_flags = jax.random.uniform(retained_key, (3, 1), minval=0.6, maxval=0.8)
    token_positions = jnp.arange(DOCUMENT_TOKENS, dtype=jnp.int32)[None, :]
    token_clusters = jnp.sum(jnp.where(token_positions == cluster_positions, jnp.log(cluster_keep_flags), 0.0), axis=0)
    return (-head_decay_rates * noise_level + token_clusters[None, :]).astype(jnp.float32)


def draw_beta(key, part):
    fast_key, slow_key = jax.random.split(jax.random.fold_in(key, 5), 2)
    is_fast = head_kinds(key)
    fast_values = jnp.exp(jax.random.uniform(fast_key, (NH, H, DOCUMENT_TOKENS), minval=math.log(0.05), maxval=0.0))
    slow_values = jnp.exp(jax.random.uniform(slow_key, (NH, H, DOCUMENT_TOKENS), minval=math.log(0.001), maxval=math.log(0.01)))
    return jnp.where(is_fast[None, :, :], fast_values, slow_values).astype(jnp.float32)


def draw_keys(key, part):
    noise_key, shared_key, mix_key = jax.random.split(jax.random.fold_in(key, 11), 3)
    shared = jax.random.normal(shared_key, (1, 1, H, DK), jnp.float32)
    mixing = jax.random.uniform(mix_key, (1, 1, H, 1), minval=0.5, maxval=1.0)
    noise = jax.random.normal(noise_key, (DOCUMENT_TOKENS, NH, H, DK), jnp.float32)
    combined = jnp.clip(noise + mixing * shared, -8.0, 8.0)
    return combined.reshape(DOCUMENT_TOKENS, NH, H * DK).astype(jnp.bfloat16)


def touch_ends(array, stream_key, smallest, high):
    dims = array.shape
    place = [jax.random.randint(jax.random.fold_in(stream_key, axis), (), 0, dims[axis]) for axis in range(len(dims))]
    array = array.at[tuple(place)].set(smallest)
    longest = dims.index(max(dims))
    place[longest] = (place[longest] + 1) % dims[longest]
    return array.at[tuple(place)].set(high)


def block_levels(rng, shape, cuts, least, high):
    loudness, own = 1.0, jax.random.fold_in(rng, 6)
    for axis_at, blocks in cuts:
        draws = jnp.exp(jax.random.uniform(jax.random.fold_in(own, axis_at), (blocks,), jnp.float32, least / len(cuts), high / len(cuts)))
        loudness = loudness * jnp.repeat(draws, shape[axis_at] // blocks).reshape([-1 if axis == axis_at else 1 for axis in range(len(shape))])
    return loudness


def bell_draw(key, shape, scale, reach, cuts=(), kind=jnp.bfloat16):
    array = scale * jax.random.normal(key, shape, jnp.float32)
    if cuts:
        array = array * block_levels(key, shape, cuts, -0.22, 0.18)
    return jnp.clip(array, -reach, reach).astype(kind)


def setup_inputs(seed: int = 0) -> dict:
    key_list = jax.random.split(jax.random.key(seed), 10)
    query = bell_draw(key_list[0], (DOCUMENT_TOKENS, H * DK), 1.0, 6.0, ((0, 64), (1, 2)))
    keys = draw_keys(jax.random.fold_in(key_list[9], 71), 0)
    values = bell_draw(key_list[2], (DOCUMENT_TOKENS, NH, H * DV), 1.0, 6.0, ((0, 64), (2, 2)))
    beta = draw_beta(jax.random.fold_in(key_list[9], 71), 0)
    gate_log = draw_gate_log(jax.random.fold_in(key_list[9], 71), 0)
    house_count = touch_ends(jax.random.randint(key_list[5], (DOCUMENT_TOKENS,), 1, NH + 1), jax.random.fold_in(key_list[5], 1), 1, NH).astype(jnp.int32)
    out_gate = bell_draw(key_list[6], (DOCUMENT_TOKENS, H * DV), 1.0, 6.0, ((0, 64), (1, 2)))
    norm_gain = jnp.clip(1.0 + 0.18 * jax.random.normal(key_list[7], (DV,), jnp.float32), 0.1, 1.9)
    out_weight = bell_draw(key_list[8], (H * DV, D), (H * DV) ** -0.5, 0.09375, ((1, 2),))
    return {"query": query, "keys": keys, "values": values, "beta": beta, "gate_log": gate_log, "house_count": house_count, "out_gate": out_gate, "norm_gain": norm_gain, "out_weight": out_weight}


epsilon = 1e-06
highest_precision = lax.Precision.HIGHEST

def unit_rows(matrix):
    return matrix / jnp.sqrt(lax.optimization_barrier(jnp.sum(matrix * matrix, axis=-1, keepdims=True)) + epsilon)

def reference(query, keys, values, beta, gate_log, house_count, out_gate, norm_gain, out_weight):
    q_unit = unit_rows(query.astype(jnp.float32).reshape(DOCUMENT_TOKENS, H, DK))
    k_unit = unit_rows(keys.astype(jnp.float32).reshape(DOCUMENT_TOKENS, NH, H, DK))
    value_rows = values.astype(jnp.float32).reshape(DOCUMENT_TOKENS, NH, H, DV)
    active = (jnp.arange(NH, dtype=jnp.int32)[:, None] < house_count[None, :]).astype(jnp.float32)
    strength = (beta * active[:, None, :]).transpose(2, 0, 1)
    forget = jnp.exp(gate_log).T

    def advance(memory_state, inputs):
        current_query, keys_now, values_now, strength_now, forget_now = inputs
        memory_state = memory_state * forget_now[:, None, None]
        for factor_index in range(NH):
            key_vector = keys_now[factor_index]
            retrieved_values = jnp.einsum('dcm,dc->dm', memory_state, key_vector, precision=highest_precision)
            update = values_now[factor_index] - retrieved_values
            memory_state = memory_state + strength_now[factor_index][:, None, None] * key_vector[:, :, None] * update[:, None, :]
        return (memory_state, jnp.einsum('dcm,dc->dm', memory_state, current_query, precision=highest_precision))
    initial = jnp.zeros((H, DK, DV), jnp.float32)
    _, head_out = lax.scan(advance, initial, (q_unit, k_unit, value_rows, strength, forget))
    inverse_rms = 1.0 / jnp.sqrt(lax.optimization_barrier(jnp.mean(head_out * head_out, axis=-1, keepdims=True)) + epsilon)
    gate_vals = jax.nn.silu(out_gate.astype(jnp.float32).reshape(DOCUMENT_TOKENS, H, DV))
    gated = (head_out * inverse_rms * norm_gain * gate_vals).astype(jnp.bfloat16).reshape(DOCUMENT_TOKENS, H * DV)
    return jnp.dot(gated, out_weight, preferred_element_type=jnp.float32).astype(jnp.bfloat16)
```

```python
import functools

import jax
import jax.numpy as jnp
from jax import lax
from jax.experimental import pallas as pl
from jax.experimental.pallas import tpu as pltpu
from jax.sharding import Mesh
from jax.sharding import PartitionSpec as P

DK = 128
DV = 128
NH = 2
TOK = 128
STEPS = TOK * NH
SEQ = ("seq_0", "seq_1", "seq_2")
PLANE = ("seq_1", "seq_2")
GROUP = 4
epsilon = 1e-06
f32, bf16 = jnp.float32, jnp.bfloat16


def dot(a, b):
    return jnp.dot(a, b, preferred_element_type=f32)


def dot_nt(a, b):
    return lax.dot_general(a, b, (((1,), (1,)), ((), ())), preferred_element_type=f32)


def split(x):
    high = x.astype(bf16)
    return high, (x - high.astype(f32)).astype(bf16)


def across(a, b):
    return jnp.concatenate([a, b], axis=1)


def down(a, b):
    return jnp.concatenate([a, b], axis=0)


def paired(a, b):
    zero = jnp.zeros_like(a)
    return down(across(a, zero), across(zero, b))


def product(a, b):
    a_high, a_low = split(a)
    b_high, b_low = split(b)
    return dot(across(a_high, a_low), down(b_high, b_high)) + dot(a_high, b_low)


def iota(shape, dim):
    return lax.broadcasted_iota(jnp.int32, shape, dim)


def local_kernel(q_ref, k_ref, v_ref, beta_ref, gate_ref, count_ref, send_ref, qe_ref, lo_ref):
    first = pl.program_id(0) * GROUP
    heads = range(GROUP)
    token, step = iota((TOK, STEPS), 0), iota((TOK, STEPS), 1)
    highest = lax.Precision.HIGHEST

    def place(rows, chosen):
        return jnp.dot(rows, chosen.astype(f32), precision=highest, preferred_element_type=f32)

    gates = gate_ref[pl.ds(first, GROUP), :]
    count = count_ref[...]
    cum = place(gates, token * NH <= step)
    cum_tok = place(gates, iota((TOK, TOK), 0) <= iota((TOK, TOK), 1))
    strength = sum(
        place(jnp.where(j < count, beta_ref[j, pl.ds(first, GROUP), :], 0.0), step == token * NH + j)
        for j in range(NH)
    )
    end = cum[:, STEPS - 1 :]
    stacked = jnp.concatenate(
        [
            cum,
            strength,
            strength * jnp.exp(cum),
            jnp.exp(end - cum),
            jnp.zeros((128 - 4 * GROUP, STEPS), f32),
        ],
        axis=0,
    )
    columns = down(stacked[:, :128].T, stacked[:, 128:].T)
    tok_columns = jnp.concatenate(
        [cum_tok, jnp.exp(cum_tok), jnp.zeros((128 - 2 * GROUP, TOK), f32)], axis=0
    ).T

    row, lane = iota((128, 128), 0), iota((128, 128), 1)
    eye = row == lane
    strictly = row > lane
    lane16 = iota((16, 128), 1)
    group16 = lane16 // 16
    eye16 = jnp.where(iota((16, 128), 0) == lane16 % 16, 1.0, 0.0).astype(f32)
    visible = step <= token * NH + (NH - 1)

    lower, corner, right, left, q_parts = [], [], [], [], []
    for g in heads:
        cols = slice(g * 128, (g + 1) * 128)
        q, k, v = q_ref[:, cols], k_ref[:, cols], v_ref[:, cols]
        q32, k32, v32 = q.astype(f32), k.astype(f32), v.astype(f32)
        rk = lax.rsqrt(jnp.sum(k32 * k32, axis=1, keepdims=True) + epsilon)
        rq = lax.rsqrt(jnp.sum(q32 * q32, axis=1, keepdims=True) + epsilon)
        gram = dot_nt(k, k)
        scores = dot_nt(q, k)
        squares = [
            jnp.sum(jnp.where(eye, gram[a : a + 128, a : a + 128], 0.0), axis=0, keepdims=True)
            for a in (0, 128)
        ]
        rk_row = lax.rsqrt(across(*squares) + epsilon)
        c_row = cum[g : g + 1, :]
        c_col = columns[:, g : g + 1]
        b_col = columns[:, GROUP + g : GROUP + g + 1]
        be_col = columns[:, 2 * GROUP + g : 2 * GROUP + g + 1]
        f_col = columns[:, 3 * GROUP + g : 3 * GROUP + g + 1]
        ct_col = tok_columns[:, g : g + 1]
        et_col = tok_columns[:, GROUP + g : GROUP + g + 1]
        scale = b_col * rk
        weighted = lambda i, j: (
            jnp.exp(c_col[i : i + 128] - c_row[:, j : j + 128])
            * gram[i : i + 128, j : j + 128]
            * scale[i : i + 128]
            * rk_row[:, j : j + 128]
        )
        lower.append([jnp.where(strictly, weighted(a, a), 0.0) for a in (0, 128)])
        corner.append(weighted(128, 0))
        right.append(across((be_col * rk) * k32, b_col * v32))
        faded = (f_col * rk) * k32
        reads = jnp.where(visible, jnp.exp(ct_col - c_row) * scores * rq * rk_row, 0.0)
        left.append(down(across(faded[:128].T, faded[128:].T), reads))
        q_parts.append((et_col * rq) * q32)

    inverse = []
    for g in heads:
        both = []
        for part in lower[g]:
            compact = part[:16]
            for b in range(1, 8):
                compact = jnp.where(group16 == b, part[16 * b : 16 * b + 16], compact)
            solved = eye16
            for r in range(15):
                spread = jnp.take_along_axis(compact, group16 * 16 + r, axis=1)
                solved = solved - spread * solved[r : r + 1]
            both.append(
                jnp.concatenate([jnp.where(group16 == b, solved, 0.0) for b in range(8)], axis=0)
            )
        inverse.append(both)
    for size in (16, 32, 64):
        odd = (row // (2 * size) == lane // (2 * size)) & ((row // size) % 2 == 1)
        odd = odd & ((lane // size) % 2 == 0)
        for g in heads:
            one, two = inverse[g]
            picked = across(*[jnp.where(odd, part, 0.0).astype(bf16) for part in lower[g]])
            mid = dot(picked, paired(one.astype(bf16), two.astype(bf16))).astype(bf16)
            out = dot(across(one, two).astype(bf16), paired(mid[:, :128], mid[:, 128:]))
            inverse[g] = [one - out[:, :128], two - out[:, 128:]]
    for g in heads:
        one, two = inverse[g]
        low = [split(part) for part in lower[g]]
        inv = [split(one), split(two)]
        high = paired(inv[0][0], inv[1][0])
        near = (
            dot(across(low[0][0], low[1][0]), high)
            + dot(across(low[0][1], low[1][1]), high)
            + dot(across(low[0][0], low[1][0]), paired(inv[0][1], inv[1][1]))
        )
        ones = jnp.where(eye, 1.0, 0.0)
        rest = [
            (ones - part - near[:, a : a + 128]).astype(bf16)
            for part, a in ((one, 0), (two, 128))
        ]
        out = dot(across(inv[0][0], inv[1][0]), paired(*rest))
        inverse[g] = [one + out[:, :128], two + out[:, 128:]]

    tops = [product(inverse[g][0], right[g][:128]) for g in heads]
    lefts = [right[g][128:] - product(corner[g], tops[g]) for g in heads]
    bottoms = [product(inverse[g][1], lefts[g]) for g in heads]
    for g in heads:
        x_high, x_low = split(down(tops[g], bottoms[g]))
        p_high, p_low = split(left[g])
        result = dot(p_high, x_high) + dot(p_low, x_high) + dot(p_high, x_low)
        lost = 1.0 - jnp.exp(end[g : g + 1])
        send_ref[g] = across(
            result[:128, :128] + jnp.where(eye, lost, 0.0), result[:128, 128:]
        ).astype(bf16)
        cols = slice(g * 128, (g + 1) * 128)
        qe_ref[:, cols] = q_parts[g] - result[128:, :128]
        lo_ref[:, cols] = result[128:, 128:]


def local_part(query, keys, values, beta, gate_log, count):
    heads = gate_log.shape[0]
    wide = GROUP * 128
    whole = lambda shape: pl.BlockSpec(shape, lambda i: (0,) * len(shape))
    return pl.pallas_call(
        local_kernel,
        grid=(heads // GROUP,),
        in_specs=[
            pl.BlockSpec((TOK, wide), lambda i: (0, i)),
            pl.BlockSpec((STEPS, wide), lambda i: (0, i)),
            pl.BlockSpec((STEPS, wide), lambda i: (0, i)),
            whole(beta.shape),
            whole(gate_log.shape),
            whole(count.shape),
        ],
        out_specs=[
            pl.BlockSpec((GROUP, 128, 256), lambda i: (i, 0, 0)),
            pl.BlockSpec((TOK, wide), lambda i: (0, i)),
            pl.BlockSpec((TOK, wide), lambda i: (0, i)),
        ],
        out_shape=[
            jax.ShapeDtypeStruct((heads, 128, 256), bf16),
            jax.ShapeDtypeStruct((TOK, heads * 128), f32),
            jax.ShapeDtypeStruct((TOK, heads * 128), f32),
        ],
        compiler_params=pltpu.CompilerParams(vmem_limit_bytes=50 * 1024 * 1024),
        name="local",
    )(query, keys, values, beta, gate_log, count)


def joined(later, earlier):
    f_high, f_low = split(later[:, :128])
    e_high, e_low = split(earlier)
    moved = dot(across(f_high, f_low), down(e_high, e_high)) + dot(f_high, e_low)
    return earlier + later - moved


def total_kernel(pieces_ref, total_ref):
    level = [pieces_ref[c].astype(f32) for c in range(pieces_ref.shape[0])]
    while len(level) > 1:
        level = [joined(level[i + 1], level[i]) for i in range(0, len(level), 2)]
    total_ref[...] = level[0].astype(bf16)


def prefix_kernel(pieces_ref, mult_ref, add_ref):
    so_far = jnp.zeros((128, 256), f32)
    for c in range(pieces_ref.shape[0]):
        high, low = split(so_far[:, :128])
        mult_ref[c] = across(high, low)
        add_ref[c] = so_far[:, 128:]
        piece = pieces_ref[c]
        factor = piece[:, :128]
        high, low = split(so_far)
        moved = dot(across(factor, factor), down(high, low))
        so_far = so_far + piece.astype(f32) - moved


def states_kernel(one_ref, two_ref, three_ref, mult_ref, add_ref, out_ref):
    state = three_ref[:, 128:].astype(f32)
    for ref in (two_ref, one_ref):
        high, low = split(state)
        factor = ref[:, :128]
        state = state + ref[:, 128:].astype(f32) - dot(across(factor, factor), down(high, low))
    high, low = split(state)
    twice = down(high, high)
    for c in range(mult_ref.shape[0]):
        mult = mult_ref[c]
        moved = dot(mult, twice) + dot(mult[:, :128], low)
        out_ref[c] = (state + add_ref[c] - moved).astype(bf16)


def read_kernel(qe_ref, lo_ref, state_ref, gate_ref, gain_ref, out_ref):
    for g in range(state_ref.shape[0]):
        cols = slice(g * 128, (g + 1) * 128)
        high, low = split(qe_ref[:, cols])
        state = state_ref[g]
        out = lo_ref[:, cols] + dot(across(high, low), down(state, state))
        inverse_rms = lax.rsqrt(jnp.mean(out * out, axis=1, keepdims=True) + epsilon)
        gate = gate_ref[:, cols].astype(f32)
        silu = gate / (1.0 + jnp.exp(-gate))
        out_ref[:, cols] = (out * inverse_rms * gain_ref[...] * silu).astype(bf16)


def read_part(query_eff, local_out, states, out_gate, norm_gain):
    heads = states.shape[0]
    wide = GROUP * 128
    block = pl.BlockSpec((TOK, wide), lambda i: (0, i))
    return pl.pallas_call(
        read_kernel,
        grid=(heads // GROUP,),
        in_specs=[
            block,
            block,
            pl.BlockSpec((GROUP, 128, 128), lambda i: (i, 0, 0)),
            block,
            pl.BlockSpec((1, 128), lambda i: (0, 0)),
        ],
        out_specs=block,
        out_shape=jax.ShapeDtypeStruct(query_eff.shape, bf16),
        name="read",
    )(query_eff, local_out, states, out_gate, norm_gain.reshape(1, DV))


def own_kernel(half_ref, rows_ref, weight_ref, out_ref):
    out_ref[...] = dot(rows_ref[...], weight_ref[...])


def other_kernel(half_ref, rows_ref, weight_ref, first_ref, out_ref):
    out_ref[...] = (first_ref[...] + dot(rows_ref[...], weight_ref[...])).astype(bf16)


def half_projection(half, rows, weight, first=None):
    depth, columns = rows.shape[1], weight.shape[1]
    wide = 512
    block = pl.BlockSpec((TOK, wide), lambda i, half: (0, i))
    specs = [
        pl.BlockSpec((TOK, depth), lambda i, half: (0, 0)),
        pl.BlockSpec((depth, wide), lambda i, half: (half[0], i)),
    ]
    args = [half, rows, weight]
    if first is not None:
        specs.append(block)
        args.append(first)
    return pl.pallas_call(
        own_kernel if first is None else other_kernel,
        grid_spec=pltpu.PrefetchScalarGridSpec(
            num_scalar_prefetch=1, grid=(columns // wide,), in_specs=specs, out_specs=block
        ),
        out_shape=jax.ShapeDtypeStruct((TOK, columns), f32 if first is None else bf16),
        cost_estimate=pl.CostEstimate(
            flops=2 * TOK * depth * columns, bytes_accessed=2 * depth * columns, transcendentals=0
        ),
        name="own_half" if first is None else "other_half",
    )(*args)


def shards(query, keys, values, beta, gate_log, house_count, out_gate, norm_gain, out_weight):
    heads = query.shape[1] // DK
    pieces, query_eff, local_out = local_part(
        query,
        keys.reshape(STEPS, heads * DK),
        values.reshape(STEPS, heads * DV),
        beta,
        gate_log,
        house_count.reshape(1, TOK),
    )
    mine = lax.all_to_all(pieces, PLANE, 0, 0, tiled=True)
    chunks = mine.shape[0]
    total = pl.pallas_call(
        total_kernel, out_shape=jax.ShapeDtypeStruct((128, 256), bf16), name="total"
    )(mine)
    planes = lax.axis_size("seq_0")
    before = [
        lax.ppermute(total, "seq_0", [(a, a + s) for a in range(planes - s)])
        for s in range(1, planes)
    ]
    mult, add = pl.pallas_call(
        prefix_kernel,
        out_shape=[
            jax.ShapeDtypeStruct((chunks, 128, 256), bf16),
            jax.ShapeDtypeStruct((chunks, 128, 128), f32),
        ],
        cost_estimate=pl.CostEstimate(
            flops=2 * chunks * 128 * 256 * 256, bytes_accessed=1 << 22, transcendentals=0
        ),
        name="prefix",
    )(mine)
    states = pl.pallas_call(
        states_kernel,
        out_shape=jax.ShapeDtypeStruct((chunks, 128, 128), bf16),
        name="states",
    )(*before, mult, add)
    states = lax.all_to_all(states, PLANE, 0, 0, tiled=True)
    gated = read_part(query_eff, local_out, states, out_gate, norm_gain)
    other = lax.ppermute(gated, "head", [(0, 1), (1, 0)])
    half = lax.axis_index("head").reshape(1).astype(jnp.int32)
    partial = half_projection(half, gated, out_weight)
    return half_projection(1 - half, other, out_weight, partial)


def solution(mesh):
    finer = Mesh(
        mesh.devices.reshape(4, 4, 4, mesh.shape["head"]), ("seq_0", "seq_1", "seq_2", "head")
    )
    in_specs = (
        P(SEQ, "head"),
        P(SEQ, None, "head"),
        P(SEQ, None, "head"),
        P(None, "head", SEQ),
        P("head", SEQ),
        P(SEQ),
        P(SEQ, "head"),
        P(),
        P(None, "head"),
    )
    out_specs = P(SEQ, "head")
    return jax.shard_map(
        shards, mesh=finer, in_specs=in_specs, out_specs=out_specs, check_vma=False
    )
```

```python
import functools

import jax
import jax.numpy as jnp
from jax import lax
from jax.experimental import pallas as pl
from jax.experimental.pallas import tpu as pltpu
from jax.sharding import Mesh
from jax.sharding import PartitionSpec as P

DK = 128
DV = 128
NH = 2
TOK = 128
STEPS = TOK * NH
SEQ = ("seq_0", "seq_1", "seq_2")
PLANE = ("seq_1", "seq_2")
GROUP = 8
MIB = 1024 * 1024
epsilon = 1e-06
f32, bf16 = jnp.float32, jnp.bfloat16


def dot(a, b):
    return jnp.dot(a, b, preferred_element_type=f32)


def dot_nt(a, b):
    return lax.dot_general(a, b, (((1,), (1,)), ((), ())), preferred_element_type=f32)


def split(x):
    high = x.astype(bf16)
    return high, (x - high.astype(f32)).astype(bf16)


def across(a, b):
    return jnp.concatenate([a, b], axis=1)


def down(a, b):
    return jnp.concatenate([a, b], axis=0)


def paired(a, b):
    zero = jnp.zeros_like(a)
    return down(across(a, zero), across(zero, b))


def product(a, b):
    a_high, a_low = split(a)
    b_high, b_low = split(b)
    return dot(across(a_high, a_low), down(b_high, b_high)) + dot(a_high, b_low)


def in_hbm(x):
    return pltpu.with_memory_space_constraint(x, pltpu.HBM)


def iota(shape, dim):
    return lax.broadcasted_iota(jnp.int32, shape, dim)


def local_kernel(q_ref, k_ref, v_ref, beta_ref, gate_ref, count_ref, send_ref, qe_ref, lo_ref):
    first = pl.program_id(0) * GROUP
    heads = range(GROUP)
    token, step = iota((TOK, STEPS), 0), iota((TOK, STEPS), 1)
    highest = lax.Precision.HIGHEST

    def place(rows, chosen):
        return jnp.dot(rows, chosen.astype(f32), precision=highest, preferred_element_type=f32)

    gates = gate_ref[pl.ds(first, GROUP), :]
    count = count_ref[...]
    cum = place(gates, token * NH <= step)
    cum_tok = place(gates, iota((TOK, TOK), 0) <= iota((TOK, TOK), 1))
    strength = sum(
        place(jnp.where(j < count, beta_ref[j, pl.ds(first, GROUP), :], 0.0), step == token * NH + j)
        for j in range(NH)
    )
    end = cum[:, STEPS - 1 :]
    stacked = jnp.concatenate(
        [
            cum,
            strength,
            strength * jnp.exp(cum),
            jnp.exp(end - cum),
            jnp.zeros((128 - 4 * GROUP, STEPS), f32),
        ],
        axis=0,
    )
    columns = down(stacked[:, :128].T, stacked[:, 128:].T)
    tok_columns = jnp.concatenate(
        [cum_tok, jnp.exp(cum_tok), jnp.zeros((128 - 2 * GROUP, TOK), f32)], axis=0
    ).T

    row, lane = iota((128, 128), 0), iota((128, 128), 1)
    eye = row == lane
    strictly = row > lane
    lane16 = iota((16, 128), 1)
    group16 = lane16 // 16
    eye16 = jnp.where(iota((16, 128), 0) == lane16 % 16, 1.0, 0.0).astype(f32)
    visible = step <= token * NH + (NH - 1)

    lower, corner, right, left, q_parts = [], [], [], [], []
    for g in heads:
        cols = slice(g * 128, (g + 1) * 128)
        q = q_ref[:, cols]
        k, v = (ref[:, :, cols].reshape(STEPS, 128) for ref in (k_ref, v_ref))
        q32, k32, v32 = q.astype(f32), k.astype(f32), v.astype(f32)
        rk = lax.rsqrt(jnp.sum(k32 * k32, axis=1, keepdims=True) + epsilon)
        rq = lax.rsqrt(jnp.sum(q32 * q32, axis=1, keepdims=True) + epsilon)
        gram = dot_nt(k, k)
        scores = dot_nt(q, k)
        squares = [
            jnp.sum(jnp.where(eye, gram[a : a + 128, a : a + 128], 0.0), axis=0, keepdims=True)
            for a in (0, 128)
        ]
        rk_row = lax.rsqrt(across(*squares) + epsilon)
        c_row = cum[g : g + 1, :]
        c_col = columns[:, g : g + 1]
        b_col = columns[:, GROUP + g : GROUP + g + 1]
        be_col = columns[:, 2 * GROUP + g : 2 * GROUP + g + 1]
        f_col = columns[:, 3 * GROUP + g : 3 * GROUP + g + 1]
        ct_col = tok_columns[:, g : g + 1]
        et_col = tok_columns[:, GROUP + g : GROUP + g + 1]
        scale = b_col * rk
        weighted = lambda i, j: (
            jnp.exp(c_col[i : i + 128] - c_row[:, j : j + 128])
            * gram[i : i + 128, j : j + 128]
            * scale[i : i + 128]
            * rk_row[:, j : j + 128]
        )
        lower.append([jnp.where(strictly, weighted(a, a), 0.0) for a in (0, 128)])
        corner.append(weighted(128, 0))
        right.append(across((be_col * rk) * k32, b_col * v32))
        faded = (f_col * rk) * k32
        reads = jnp.where(visible, jnp.exp(ct_col - c_row) * scores * rq * rk_row, 0.0)
        left.append(down(across(faded[:128].T, faded[128:].T), reads))
        q_parts.append((et_col * rq) * q32)

    inverse = []
    for g in heads:
        both = []
        for part in lower[g]:
            compact = part[:16]
            for b in range(1, 8):
                compact = jnp.where(group16 == b, part[16 * b : 16 * b + 16], compact)
            solved = eye16
            for r in range(15):
                spread = jnp.take_along_axis(compact, group16 * 16 + r, axis=1)
                solved = solved - spread * solved[r : r + 1]
            both.append(
                jnp.concatenate([jnp.where(group16 == b, solved, 0.0) for b in range(8)], axis=0)
            )
        inverse.append(both)
    for size in (16, 32, 64):
        odd = (row // (2 * size) == lane // (2 * size)) & ((row // size) % 2 == 1)
        odd = odd & ((lane // size) % 2 == 0)
        for g in heads:
            one, two = inverse[g]
            picked = across(*[jnp.where(odd, part, 0.0).astype(bf16) for part in lower[g]])
            mid = dot(picked, paired(one.astype(bf16), two.astype(bf16))).astype(bf16)
            out = dot(across(one, two).astype(bf16), paired(mid[:, :128], mid[:, 128:]))
            inverse[g] = [one - out[:, :128], two - out[:, 128:]]
    for g in heads:
        one, two = inverse[g]
        low = [split(part) for part in lower[g]]
        inv = [split(one), split(two)]
        high = paired(inv[0][0], inv[1][0])
        near = (
            dot(across(low[0][0], low[1][0]), high)
            + dot(across(low[0][1], low[1][1]), high)
            + dot(across(low[0][0], low[1][0]), paired(inv[0][1], inv[1][1]))
        )
        ones = jnp.where(eye, 1.0, 0.0)
        rest = [
            (ones - part - near[:, a : a + 128]).astype(bf16)
            for part, a in ((one, 0), (two, 128))
        ]
        out = dot(across(inv[0][0], inv[1][0]), paired(*rest))
        inverse[g] = [one + out[:, :128], two + out[:, 128:]]

    tops = [product(inverse[g][0], right[g][:128]) for g in heads]
    lefts = [right[g][128:] - product(corner[g], tops[g]) for g in heads]
    bottoms = [product(inverse[g][1], lefts[g]) for g in heads]
    for g in heads:
        x_high, x_low = split(down(tops[g], bottoms[g]))
        p_high, p_low = split(left[g])
        result = dot(p_high, x_high) + dot(p_low, x_high) + dot(p_high, x_low)
        lost = 1.0 - jnp.exp(end[g : g + 1])
        send_ref[g] = across(
            result[:128, :128] + jnp.where(eye, lost, 0.0), result[:128, 128:]
        ).astype(bf16)
        cols = slice(g * 128, (g + 1) * 128)
        qe_ref[:, cols] = q_parts[g] - result[128:, :128]
        lo_ref[:, cols] = result[128:, 128:]


def local_part(query, keys, values, beta, gate_log, count):
    heads = gate_log.shape[0]
    wide = GROUP * 128
    whole = lambda shape: pl.BlockSpec(shape, lambda i: (0,) * len(shape))
    return pl.pallas_call(
        local_kernel,
        grid=(heads // GROUP,),
        in_specs=[
            pl.BlockSpec((TOK, wide), lambda i: (0, i)),
            pl.BlockSpec((TOK, NH, wide), lambda i: (0, 0, i)),
            pl.BlockSpec((TOK, NH, wide), lambda i: (0, 0, i)),
            whole(beta.shape),
            whole(gate_log.shape),
            whole(count.shape),
        ],
        out_specs=[
            pl.BlockSpec((GROUP, 128, 256), lambda i: (i, 0, 0)),
            pl.BlockSpec((TOK, wide), lambda i: (0, i)),
            pl.BlockSpec((TOK, wide), lambda i: (0, i)),
        ],
        out_shape=[
            jax.ShapeDtypeStruct((heads, 128, 256), bf16),
            jax.ShapeDtypeStruct((TOK, heads * 128), f32),
            jax.ShapeDtypeStruct((TOK, heads * 128), f32),
        ],
        name="local",
    )(query, keys, values, beta, gate_log, count)


def joined(later, earlier):
    f_high, f_low = split(later[:, :128])
    e_high, e_low = split(earlier)
    moved = dot(across(f_high, f_low), down(e_high, e_high)) + dot(f_high, e_low)
    return earlier + later - moved


def total_kernel(pieces_ref, total_ref, mult_ref, add_ref):
    level = [pieces_ref[c].astype(f32) for c in range(pieces_ref.shape[0])]
    kept = []
    while len(level) > 1:
        level = [joined(level[i + 1], level[i]) for i in range(0, len(level), 2)]
        kept = level[0::2] + kept
    total_ref[...] = kept[0].astype(bf16)
    for i, node in enumerate(kept[1:]):
        mult_ref[i] = across(*split(node[:, :128]))
        add_ref[i] = node[:, 128:]


def states_kernel(one_ref, two_ref, three_ref, pieces_ref, mult_ref, add_ref, out_ref):
    state = three_ref[:, 128:].astype(f32)

    def stepped(piece, state):
        factor = piece[:, :128]
        high, low = split(state)
        moved = dot(across(factor, factor), down(high, low))
        return state + piece[:, 128:].astype(f32) - moved

    for ref in (two_ref, one_ref):
        state = stepped(ref[...], state)
    starts, node = [state], 0
    while 2 * len(starts) < pieces_ref.shape[0]:
        finer = []
        for state in starts:
            high, low = split(state)
            mult = mult_ref[node]
            moved = dot(mult, down(high, high)) + dot(mult[:, :128], low)
            finer += [state, state + add_ref[node] - moved]
            node += 1
        starts = finer
    for i, state in enumerate(starts):
        out_ref[2 * i] = state.astype(bf16)
        out_ref[2 * i + 1] = stepped(pieces_ref[2 * i], state).astype(bf16)


def read_kernel(qe_ref, lo_ref, state_ref, gate_ref, gain_ref, out_ref):
    for g in range(state_ref.shape[0]):
        cols = slice(g * 128, (g + 1) * 128)
        high, low = split(qe_ref[:, cols])
        state = state_ref[g]
        out = lo_ref[:, cols] + dot(across(high, low), down(state, state))
        inverse_rms = lax.rsqrt(jnp.mean(out * out, axis=1, keepdims=True) + epsilon)
        gate = gate_ref[:, cols].astype(f32)
        silu = gate / (1.0 + jnp.exp(-gate))
        out_ref[:, cols] = (out * inverse_rms * gain_ref[...] * silu).astype(bf16)


def read_part(query_eff, local_out, states, out_gate, norm_gain):
    heads = states.shape[0]
    wide = GROUP * 128
    block = pl.BlockSpec((TOK, wide), lambda i: (0, i))
    return pl.pallas_call(
        read_kernel,
        grid=(heads // GROUP,),
        in_specs=[
            block,
            block,
            pl.BlockSpec((GROUP, 128, 128), lambda i: (i, 0, 0)),
            block,
            pl.BlockSpec((1, 128), lambda i: (0, 0)),
        ],
        out_specs=block,
        out_shape=jax.ShapeDtypeStruct(query_eff.shape, bf16),
        compiler_params=pltpu.CompilerParams(vmem_limit_bytes=32 * MIB),
        name="read",
    )(*map(in_hbm, (query_eff, local_out, states, out_gate, norm_gain.reshape(1, DV))))


def own_kernel(half_ref, rows_ref, weight_ref, out_ref):
    out_ref[...] = dot(rows_ref[...], weight_ref[...])


def other_kernel(half_ref, rows_ref, weight_ref, first_ref, out_ref):
    out_ref[...] = (first_ref[...] + dot(rows_ref[...], weight_ref[...])).astype(bf16)


def half_projection(half, rows, weight, first=None):
    depth, columns = rows.shape[1], weight.shape[1]
    wide = 1024
    block = pl.BlockSpec((TOK, wide), lambda i, half: (0, i))
    specs = [
        pl.BlockSpec((TOK, depth), lambda i, half: (0, 0)),
        pl.BlockSpec((depth, wide), lambda i, half: (half[0], i)),
    ]
    args = [half, rows, in_hbm(weight)]
    if first is not None:
        specs.append(block)
        args.append(first)
    return pl.pallas_call(
        own_kernel if first is None else other_kernel,
        grid_spec=pltpu.PrefetchScalarGridSpec(
            num_scalar_prefetch=1, grid=(columns // wide,), in_specs=specs, out_specs=block
        ),
        out_shape=jax.ShapeDtypeStruct((TOK, columns), f32 if first is None else bf16),
        cost_estimate=pl.CostEstimate(
            flops=2 * TOK * depth * columns, bytes_accessed=2 * depth * columns, transcendentals=0
        ),
        compiler_params=pltpu.CompilerParams(vmem_limit_bytes=32 * MIB),
        name="own_half" if first is None else "other_half",
    )(*args)


def shards(query, keys, values, beta, gate_log, house_count, out_gate, norm_gain, out_weight):
    heads = query.shape[1] // DK
    pieces, query_eff, local_out = local_part(
        query,
        keys,
        values,
        beta,
        gate_log,
        house_count.reshape(1, TOK),
    )
    mine = lax.all_to_all(pieces, PLANE, 0, 0, tiled=True)
    chunks = mine.shape[0]
    nodes = chunks // 2 - 1
    total, mult, add = pl.pallas_call(
        total_kernel,
        out_shape=[
            jax.ShapeDtypeStruct((128, 256), bf16),
            jax.ShapeDtypeStruct((nodes, 128, 256), bf16),
            jax.ShapeDtypeStruct((nodes, 128, 128), f32),
        ],
        name="total",
    )(mine)
    planes = lax.axis_size("seq_0")
    before = [
        lax.ppermute(total, "seq_0", [(a, a + s) for a in range(planes - s)])
        for s in range(1, planes)
    ]
    states = pl.pallas_call(
        states_kernel,
        out_shape=jax.ShapeDtypeStruct((chunks, 128, 128), bf16),
        compiler_params=pltpu.CompilerParams(vmem_limit_bytes=32 * MIB),
        name="states",
    )(*before, *map(in_hbm, (mine, mult, add)))
    states = lax.all_to_all(states, PLANE, 0, 0, tiled=True)
    gated = read_part(query_eff, local_out, states, out_gate, norm_gain)
    other = lax.ppermute(gated, "head", [(0, 1), (1, 0)])
    half = lax.axis_index("head").reshape(1).astype(jnp.int32)
    partial = half_projection(half, gated, out_weight)
    return half_projection(1 - half, other, out_weight, partial)


def solution(mesh):
    finer = Mesh(
        mesh.devices.reshape(4, 4, 4, mesh.shape["head"]), ("seq_0", "seq_1", "seq_2", "head")
    )
    in_specs = (
        P(SEQ, "head"),
        P(SEQ, None, "head"),
        P(SEQ, None, "head"),
        P(None, "head", SEQ),
        P("head", SEQ),
        P(SEQ),
        P(SEQ, "head"),
        P(),
        P(None, "head"),
    )
    out_specs = P(SEQ, "head")
    return jax.shard_map(
        shards, mesh=finer, in_specs=in_specs, out_specs=out_specs, check_vma=False
    )
```

```python
import functools

import jax
import jax.numpy as jnp
from jax import lax
from jax.experimental import pallas as pl
from jax.experimental.pallas import tpu as pltpu
from jax.sharding import Mesh
from jax.sharding import PartitionSpec as P

DK = 128
DV = 128
NH = 2
TOK = 128
STEPS = TOK * NH
SEQ = ("seq_0", "seq_1", "seq_2")
PLANE = ("seq_1", "seq_2")
GROUP = 8
SKEW = 1
ABREAST = 1
MIB = 1024 * 1024
epsilon = 1e-06
f32, bf16 = jnp.float32, jnp.bfloat16


def dot(a, b):
    return jnp.dot(a, b, preferred_element_type=f32)


def dot_nt(a, b):
    return lax.dot_general(a, b, (((1,), (1,)), ((), ())), preferred_element_type=f32)


def split(x):
    high = x.astype(bf16)
    return high, (x - high.astype(f32)).astype(bf16)


def across(a, b):
    return jnp.concatenate([a, b], axis=1)


def down(a, b):
    return jnp.concatenate([a, b], axis=0)


def paired(a, b):
    zero = jnp.zeros_like(a)
    return down(across(a, zero), across(zero, b))


def product(a, b):
    a_high, a_low = split(a)
    b_high, b_low = split(b)
    return dot(across(a_high, a_low), down(b_high, b_high)) + dot(a_high, b_low)


def in_hbm(x):
    return pltpu.with_memory_space_constraint(x, pltpu.HBM)


def iota(shape, dim):
    return lax.broadcasted_iota(jnp.int32, shape, dim)


def local_kernel(q_ref, k_ref, v_ref, beta_ref, gate_ref, count_ref, send_ref, qe_ref, lo_ref):
    first = pl.program_id(0) * GROUP
    heads = range(GROUP)
    token, step = iota((TOK, STEPS), 0), iota((TOK, STEPS), 1)
    highest = lax.Precision.HIGHEST

    def place(rows, chosen):
        return jnp.dot(rows, chosen.astype(f32), precision=highest, preferred_element_type=f32)

    gates = gate_ref[pl.ds(first, GROUP), :]
    count = count_ref[...]
    cum = place(gates, token * NH <= step)
    cum_tok = place(gates, iota((TOK, TOK), 0) <= iota((TOK, TOK), 1))
    strength = sum(
        place(jnp.where(j < count, beta_ref[j, pl.ds(first, GROUP), :], 0.0), step == token * NH + j)
        for j in range(NH)
    )
    end = cum[:, STEPS - 1 :]
    stacked = jnp.concatenate(
        [
            cum,
            strength,
            strength * jnp.exp(cum),
            jnp.exp(end - cum),
            jnp.zeros((128 - 4 * GROUP, STEPS), f32),
        ],
        axis=0,
    )
    columns = down(stacked[:, :128].T, stacked[:, 128:].T)
    tok_columns = jnp.concatenate(
        [cum_tok, jnp.exp(cum_tok), jnp.zeros((128 - 2 * GROUP, TOK), f32)], axis=0
    ).T

    row, lane = iota((128, 128), 0), iota((128, 128), 1)
    eye = row == lane
    strictly = row > lane
    lane16 = iota((16, 128), 1)
    group16 = lane16 // 16
    eye16 = jnp.where(iota((16, 128), 0) == lane16 % 16, 1.0, 0.0).astype(f32)
    visible = step <= token * NH + (NH - 1)

    ones = jnp.where(eye, 1.0, 0.0)
    levels = []
    for size in (16, 32, 64):
        odd = (row // (2 * size) == lane // (2 * size)) & ((row // size) % 2 == 1)
        levels.append(jnp.where(odd & ((lane // size) % 2 == 0), 1.0, 0.0).astype(bf16))
    spread_from = [group16[:8] * 16 + r for r in range(15)]

    def one_head(g):
        cols = slice(g * 128, (g + 1) * 128)
        q = q_ref[:, cols]
        k, v = (ref[:, :, cols].reshape(STEPS, 128) for ref in (k_ref, v_ref))
        q32, k32, v32 = q.astype(f32), k.astype(f32), v.astype(f32)
        gram = dot_nt(k, k)
        scores = dot_nt(q, k)
        rk = lax.rsqrt(jnp.sum(k32 * k32, axis=1, keepdims=True) + epsilon)
        rq = lax.rsqrt(jnp.sum(q32 * q32, axis=1, keepdims=True) + epsilon)
        yield
        squares = [
            jnp.sum(jnp.where(eye, gram[a : a + 128, a : a + 128], 0.0), axis=0, keepdims=True)
            for a in (0, 128)
        ]
        rk_row = lax.rsqrt(across(*squares) + epsilon)
        c_row = cum[g : g + 1, :]
        c_col = columns[:, g : g + 1]
        b_col = columns[:, GROUP + g : GROUP + g + 1]
        be_col = columns[:, 2 * GROUP + g : 2 * GROUP + g + 1]
        f_col = columns[:, 3 * GROUP + g : 3 * GROUP + g + 1]
        ct_col = tok_columns[:, g : g + 1]
        et_col = tok_columns[:, GROUP + g : GROUP + g + 1]
        scale = b_col * rk

        def weighted(i, j):
            return (
                jnp.exp(c_col[i : i + 128] - c_row[:, j : j + 128])
                * gram[i : i + 128, j : j + 128]
                * scale[i : i + 128]
                * rk_row[:, j : j + 128]
            )

        lower = [jnp.where(strictly, weighted(a, a), 0.0) for a in (0, 128)]
        yield
        solved, compact = [eye16, eye16], []
        for part in lower:
            picked = part[:16]
            for b in range(1, 8):
                picked = jnp.where(group16 == b, part[16 * b : 16 * b + 16], picked)
            compact.append(picked)
        solved, compact = [[x[:8], x[8:]] for x in solved], [[x[:8], x[8:]] for x in compact]
        for r in range(15):
            for i in range(2):
                source = solved[i][r // 8][r % 8 : r % 8 + 1]
                for part in range((r + 1) // 8, 2):
                    spread = jnp.take_along_axis(compact[i][part], spread_from[r], axis=1)
                    solved[i][part] = solved[i][part] - spread * source
            if r % 5 == 4:
                yield
        one, two = [
            jnp.concatenate([jnp.where(group16 == b, down(*x), 0.0) for b in range(8)], axis=0)
            for x in solved
        ]
        low = [split(part) for part in lower]
        for odd in levels:
            picked = across(low[0][0] * odd, low[1][0] * odd)
            narrow = one.astype(bf16), two.astype(bf16)
            mid = dot(picked, paired(*narrow)).astype(bf16)
            yield
            out = dot(across(*narrow), paired(mid[:, :128], mid[:, 128:]))
            one, two = one - out[:, :128], two - out[:, 128:]
            yield
        inv = [split(one), split(two)]
        high = paired(inv[0][0], inv[1][0])
        near = (
            dot(across(low[0][0], low[1][0]), high)
            + dot(across(low[0][1], low[1][1]), high)
            + dot(across(low[0][0], low[1][0]), paired(inv[0][1], inv[1][1]))
        )
        rest = [
            (ones - part - near[:, a : a + 128]).astype(bf16)
            for part, a in ((one, 0), (two, 128))
        ]
        yield
        out = dot(across(inv[0][0], inv[1][0]), paired(*rest))
        one, two = one + out[:, :128], two + out[:, 128:]
        yield
        right = across((be_col * rk) * k32, b_col * v32)
        top = product(one, right[:128])
        yield
        rest = right[128:] - product(weighted(128, 0), top)
        yield
        bottom = product(two, rest)
        faded = (f_col * rk) * k32
        yield
        reads = jnp.where(visible, jnp.exp(ct_col - c_row) * scores * rq * rk_row, 0.0)
        x_high, x_low = split(down(top, bottom))
        p_high, p_low = split(down(across(faded[:128].T, faded[128:].T), reads))
        result = dot(p_high, x_high) + dot(p_low, x_high) + dot(p_high, x_low)
        yield
        lost = 1.0 - jnp.exp(end[g : g + 1])
        send_ref[g] = across(
            result[:128, :128] + jnp.where(eye, lost, 0.0), result[:128, 128:]
        ).astype(bf16)
        qe_ref[:, cols] = (et_col * rq) * q32 - result[128:, :128]
        lo_ref[:, cols] = result[128:, 128:]

    waiting, running, tick = [one_head(g) for g in heads], [], 0
    while waiting or running:
        if waiting and tick % SKEW == 0:
            running.extend(waiting[:ABREAST])
            waiting = waiting[ABREAST:]
        running = [work for work in running if next(work, work) is None]
        tick += 1


def local_part(query, keys, values, beta, gate_log, count):
    heads = gate_log.shape[0]
    wide = GROUP * 128
    whole = lambda shape: pl.BlockSpec(shape, lambda i: (0,) * len(shape))
    return pl.pallas_call(
        local_kernel,
        grid=(heads // GROUP,),
        in_specs=[
            pl.BlockSpec((TOK, wide), lambda i: (0, i)),
            pl.BlockSpec((TOK, NH, wide), lambda i: (0, 0, i)),
            pl.BlockSpec((TOK, NH, wide), lambda i: (0, 0, i)),
            whole(beta.shape),
            whole(gate_log.shape),
            whole(count.shape),
        ],
        out_specs=[
            pl.BlockSpec((GROUP, 128, 256), lambda i: (i, 0, 0)),
            pl.BlockSpec((TOK, wide), lambda i: (0, i)),
            pl.BlockSpec((TOK, wide), lambda i: (0, i)),
        ],
        out_shape=[
            jax.ShapeDtypeStruct((heads, 128, 256), bf16),
            jax.ShapeDtypeStruct((TOK, heads * 128), f32),
            jax.ShapeDtypeStruct((TOK, heads * 128), f32),
        ],
        name="local",
    )(query, keys, values, beta, gate_log, count)


def joined(later, earlier):
    f_high, f_low = split(later[:, :128])
    e_high, e_low = split(earlier)
    moved = dot(across(f_high, f_low), down(e_high, e_high)) + dot(f_high, e_low)
    return earlier + later - moved


def total_kernel(pieces_ref, total_ref, mult_ref, add_ref):
    level = [pieces_ref[c].astype(f32) for c in range(pieces_ref.shape[0])]
    kept = []
    while len(level) > 1:
        level = [joined(level[i + 1], level[i]) for i in range(0, len(level), 2)]
        kept = level[0::2] + kept
    total_ref[...] = kept[0].astype(bf16)
    for i, node in enumerate(kept[1:]):
        mult_ref[i] = across(*split(node[:, :128]))
        add_ref[i] = node[:, 128:]


def states_kernel(one_ref, two_ref, three_ref, pieces_ref, mult_ref, add_ref, out_ref):
    state = three_ref[:, 128:].astype(f32)

    def stepped(piece, state):
        factor = piece[:, :128]
        high, low = split(state)
        moved = dot(across(factor, factor), down(high, low))
        return state + piece[:, 128:].astype(f32) - moved

    for ref in (two_ref, one_ref):
        state = stepped(ref[...], state)
    starts, node = [state], 0
    while 2 * len(starts) < pieces_ref.shape[0]:
        finer = []
        for state in starts:
            high, low = split(state)
            mult = mult_ref[node]
            moved = dot(mult, down(high, high)) + dot(mult[:, :128], low)
            finer += [state, state + add_ref[node] - moved]
            node += 1
        starts = finer
    for i, state in enumerate(starts):
        out_ref[2 * i] = state.astype(bf16)
        out_ref[2 * i + 1] = stepped(pieces_ref[2 * i], state).astype(bf16)


def read_kernel(qe_ref, lo_ref, state_ref, gate_ref, gain_ref, out_ref):
    for g in range(state_ref.shape[0]):
        cols = slice(g * 128, (g + 1) * 128)
        high, low = split(qe_ref[:, cols])
        state = state_ref[g]
        out = lo_ref[:, cols] + dot(across(high, low), down(state, state))
        inverse_rms = lax.rsqrt(jnp.mean(out * out, axis=1, keepdims=True) + epsilon)
        gate = gate_ref[:, cols].astype(f32)
        silu = gate / (1.0 + jnp.exp(-gate))
        out_ref[:, cols] = (out * inverse_rms * gain_ref[...] * silu).astype(bf16)


def read_part(query_eff, local_out, states, out_gate, norm_gain):
    heads = states.shape[0]
    wide = GROUP * 128
    block = pl.BlockSpec((TOK, wide), lambda i: (0, i))
    return pl.pallas_call(
        read_kernel,
        grid=(heads // GROUP,),
        in_specs=[
            block,
            block,
            pl.BlockSpec((GROUP, 128, 128), lambda i: (i, 0, 0)),
            block,
            pl.BlockSpec((1, 128), lambda i: (0, 0)),
        ],
        out_specs=block,
        out_shape=jax.ShapeDtypeStruct(query_eff.shape, bf16),
        compiler_params=pltpu.CompilerParams(vmem_limit_bytes=32 * MIB),
        name="read",
    )(*map(in_hbm, (query_eff, local_out, states, out_gate, norm_gain.reshape(1, DV))))


def own_kernel(half_ref, rows_ref, weight_ref, out_ref):
    out_ref[...] = dot(rows_ref[...], weight_ref[...])


def other_kernel(half_ref, rows_ref, weight_ref, first_ref, out_ref):
    out_ref[...] = (first_ref[...] + dot(rows_ref[...], weight_ref[...])).astype(bf16)


def half_projection(half, rows, weight, first=None):
    depth, columns = rows.shape[1], weight.shape[1]
    wide = 1024
    block = pl.BlockSpec((TOK, wide), lambda i, half: (0, i))
    specs = [
        pl.BlockSpec((TOK, depth), lambda i, half: (0, 0)),
        pl.BlockSpec((depth, wide), lambda i, half: (half[0], i)),
    ]
    args = [half, rows, in_hbm(weight)]
    if first is not None:
        specs.append(block)
        args.append(first)
    return pl.pallas_call(
        own_kernel if first is None else other_kernel,
        grid_spec=pltpu.PrefetchScalarGridSpec(
            num_scalar_prefetch=1, grid=(columns // wide,), in_specs=specs, out_specs=block
        ),
        out_shape=jax.ShapeDtypeStruct((TOK, columns), f32 if first is None else bf16),
        cost_estimate=pl.CostEstimate(
            flops=2 * TOK * depth * columns, bytes_accessed=2 * depth * columns, transcendentals=0
        ),
        compiler_params=pltpu.CompilerParams(vmem_limit_bytes=32 * MIB),
        name="own_half" if first is None else "other_half",
    )(*args)


def shards(query, keys, values, beta, gate_log, house_count, out_gate, norm_gain, out_weight):
    heads = query.shape[1] // DK
    pieces, query_eff, local_out = local_part(
        query,
        keys,
        values,
        beta,
        gate_log,
        house_count.reshape(1, TOK),
    )
    mine = lax.all_to_all(pieces, PLANE, 0, 0, tiled=True)
    chunks = mine.shape[0]
    nodes = chunks // 2 - 1
    total, mult, add = pl.pallas_call(
        total_kernel,
        out_shape=[
            jax.ShapeDtypeStruct((128, 256), bf16),
            jax.ShapeDtypeStruct((nodes, 128, 256), bf16),
            jax.ShapeDtypeStruct((nodes, 128, 128), f32),
        ],
        compiler_params=pltpu.CompilerParams(vmem_limit_bytes=32 * MIB),
        name="total",
    )(in_hbm(mine))
    planes = lax.axis_size("seq_0")
    before = [
        lax.ppermute(total, "seq_0", [(a, a + s) for a in range(planes - s)])
        for s in range(1, planes)
    ]
    states = pl.pallas_call(
        states_kernel,
        out_shape=jax.ShapeDtypeStruct((chunks, 128, 128), bf16),
        compiler_params=pltpu.CompilerParams(vmem_limit_bytes=32 * MIB),
        name="states",
    )(*before, in_hbm(mine), mult, add)
    states = lax.all_to_all(states, PLANE, 0, 0, tiled=True)
    gated = read_part(query_eff, local_out, states, out_gate, norm_gain)
    other = lax.ppermute(gated, "head", [(0, 1), (1, 0)])
    half = lax.axis_index("head").reshape(1).astype(jnp.int32)
    partial = half_projection(half, gated, out_weight)
    return half_projection(1 - half, other, out_weight, partial)


def solution(mesh):
    finer = Mesh(
        mesh.devices.reshape(4, 4, 4, mesh.shape["head"]), ("seq_0", "seq_1", "seq_2", "head")
    )
    in_specs = (
        P(SEQ, "head"),
        P(SEQ, None, "head"),
        P(SEQ, None, "head"),
        P(None, "head", SEQ),
        P("head", SEQ),
        P(SEQ),
        P(SEQ, "head"),
        P(),
        P(None, "head"),
    )
    out_specs = P(SEQ, "head")
    return jax.shard_map(
        shards, mesh=finer, in_specs=in_specs, out_specs=out_specs, check_vma=False
    )
```

```python
import functools

import jax
import jax.numpy as jnp
from jax import lax
from jax.experimental import pallas as pl
from jax.experimental.pallas import tpu as pltpu
from jax.sharding import Mesh
from jax.sharding import PartitionSpec as P

DK = 128
DV = 128
NH = 2
TOK = 128
STEPS = TOK * NH
SEQ = ("seq_0", "seq_1", "seq_2")
PLANE = ("seq_1", "seq_2")
GROUP = 8
SKEW = 1
ABREAST = 1
MIB = 1024 * 1024
epsilon = 1e-06
f32, bf16 = jnp.float32, jnp.bfloat16


def dot(a, b):
    return jnp.dot(a, b, preferred_element_type=f32)


def dot_nt(a, b):
    return lax.dot_general(a, b, (((1,), (1,)), ((), ())), preferred_element_type=f32)


def split(x):
    high = x.astype(bf16)
    return high, (x - high.astype(f32)).astype(bf16)


def across(a, b):
    return jnp.concatenate([a, b], axis=1)


def down(a, b):
    return jnp.concatenate([a, b], axis=0)


def paired(a, b):
    zero = jnp.zeros_like(a)
    return down(across(a, zero), across(zero, b))


def product(a, b):
    a_high, a_low = split(a)
    b_high, b_low = split(b)
    return dot(across(a_high, a_low), down(b_high, b_high)) + dot(a_high, b_low)


def in_hbm(x):
    return pltpu.with_memory_space_constraint(x, pltpu.HBM)


def iota(shape, dim):
    return lax.broadcasted_iota(jnp.int32, shape, dim)


def local_kernel(q_ref, k_ref, v_ref, beta_ref, gate_ref, count_ref, send_ref, qe_ref, lo_ref):
    first = pl.program_id(0) * GROUP
    heads = range(GROUP)
    token, step = iota((TOK, STEPS), 0), iota((TOK, STEPS), 1)
    highest = lax.Precision.HIGHEST

    def place(rows, chosen):
        return jnp.dot(rows, chosen.astype(f32), precision=highest, preferred_element_type=f32)

    gates = gate_ref[pl.ds(first, GROUP), :]
    count = count_ref[...]
    cum = place(gates, token * NH <= step)
    cum_tok = place(gates, iota((TOK, TOK), 0) <= iota((TOK, TOK), 1))
    strength = sum(
        place(jnp.where(j < count, beta_ref[j, pl.ds(first, GROUP), :], 0.0), step == token * NH + j)
        for j in range(NH)
    )
    end = cum[:, STEPS - 1 :]
    stacked = jnp.concatenate(
        [
            cum,
            strength,
            strength * jnp.exp(cum),
            jnp.exp(end - cum),
            jnp.zeros((128 - 4 * GROUP, STEPS), f32),
        ],
        axis=0,
    )
    columns = down(stacked[:, :128].T, stacked[:, 128:].T)
    tok_columns = jnp.concatenate(
        [cum_tok, jnp.exp(cum_tok), jnp.zeros((128 - 2 * GROUP, TOK), f32)], axis=0
    ).T

    row, lane = iota((128, 128), 0), iota((128, 128), 1)
    eye = row == lane
    strictly = row > lane
    lane16 = iota((16, 128), 1)
    group16 = lane16 // 16
    eye16 = jnp.where(iota((16, 128), 0) == lane16 % 16, 1.0, 0.0).astype(f32)
    visible = step <= token * NH + (NH - 1)

    ones = jnp.where(eye, 1.0, 0.0)
    levels = []
    for size in (16, 32, 64):
        odd = (row // (2 * size) == lane // (2 * size)) & ((row // size) % 2 == 1)
        levels.append(jnp.where(odd & ((lane // size) % 2 == 0), 1.0, 0.0).astype(bf16))
    spread_from = [group16[:8] * 16 + r for r in range(15)]

    def one_head(g):
        cols = slice(g * 128, (g + 1) * 128)
        q = q_ref[:, cols]
        k, v = (ref[:, :, cols].reshape(STEPS, 128) for ref in (k_ref, v_ref))
        q32, k32, v32 = q.astype(f32), k.astype(f32), v.astype(f32)
        gram = dot_nt(k, k)
        scores = dot_nt(q, k)
        rk = lax.rsqrt(jnp.sum(k32 * k32, axis=1, keepdims=True) + epsilon)
        rq = lax.rsqrt(jnp.sum(q32 * q32, axis=1, keepdims=True) + epsilon)
        yield
        squares = [
            jnp.sum(jnp.where(eye, gram[a : a + 128, a : a + 128], 0.0), axis=0, keepdims=True)
            for a in (0, 128)
        ]
        rk_row = lax.rsqrt(across(*squares) + epsilon)
        c_row = cum[g : g + 1, :]
        c_col = columns[:, g : g + 1]
        b_col = columns[:, GROUP + g : GROUP + g + 1]
        be_col = columns[:, 2 * GROUP + g : 2 * GROUP + g + 1]
        f_col = columns[:, 3 * GROUP + g : 3 * GROUP + g + 1]
        ct_col = tok_columns[:, g : g + 1]
        et_col = tok_columns[:, GROUP + g : GROUP + g + 1]
        scale = b_col * rk

        def weighted(i, j):
            return (
                jnp.exp(c_col[i : i + 128] - c_row[:, j : j + 128])
                * gram[i : i + 128, j : j + 128]
                * scale[i : i + 128]
                * rk_row[:, j : j + 128]
            )

        lower = [jnp.where(strictly, weighted(a, a), 0.0) for a in (0, 128)]
        yield
        solved, compact = [eye16, eye16], []
        for part in lower:
            picked = part[:16]
            for b in range(1, 8):
                picked = jnp.where(group16 == b, part[16 * b : 16 * b + 16], picked)
            compact.append(picked)
        solved, compact = [[x[:8], x[8:]] for x in solved], [[x[:8], x[8:]] for x in compact]
        for r in range(15):
            for i in range(2):
                source = solved[i][r // 8][r % 8 : r % 8 + 1]
                for part in range((r + 1) // 8, 2):
                    spread = jnp.take_along_axis(compact[i][part], spread_from[r], axis=1)
                    solved[i][part] = solved[i][part] - spread * source
            if r % 5 == 4:
                yield
        one, two = [
            jnp.concatenate([jnp.where(group16 == b, down(*x), 0.0) for b in range(8)], axis=0)
            for x in solved
        ]
        low = [split(part) for part in lower]
        for odd in levels:
            picked = across(low[0][0] * odd, low[1][0] * odd)
            narrow = one.astype(bf16), two.astype(bf16)
            mid = dot(picked, paired(*narrow)).astype(bf16)
            yield
            out = dot(across(*narrow), paired(mid[:, :128], mid[:, 128:]))
            one, two = one - out[:, :128], two - out[:, 128:]
            yield
        inv = [split(one), split(two)]
        high = paired(inv[0][0], inv[1][0])
        near = (
            dot(across(low[0][0], low[1][0]), high)
            + dot(across(low[0][1], low[1][1]), high)
            + dot(across(low[0][0], low[1][0]), paired(inv[0][1], inv[1][1]))
        )
        rest = [
            (ones - part - near[:, a : a + 128]).astype(bf16)
            for part, a in ((one, 0), (two, 128))
        ]
        yield
        out = dot(across(inv[0][0], inv[1][0]), paired(*rest))
        one, two = one + out[:, :128], two + out[:, 128:]
        yield
        right = across((be_col * rk) * k32, b_col * v32)
        top = product(one, right[:128])
        yield
        rest = right[128:] - product(weighted(128, 0), top)
        yield
        bottom = product(two, rest)
        faded = (f_col * rk) * k32
        yield
        reads = jnp.where(visible, jnp.exp(ct_col - c_row) * scores * rq * rk_row, 0.0)
        x_high, x_low = split(down(top, bottom))
        p_high, p_low = split(down(across(faded[:128].T, faded[128:].T), reads))
        result = dot(p_high, x_high) + dot(p_low, x_high) + dot(p_high, x_low)
        yield
        lost = 1.0 - jnp.exp(end[g : g + 1])
        send_ref[g] = across(
            result[:128, :128] + jnp.where(eye, lost, 0.0), result[:128, 128:]
        ).astype(bf16)
        qe_ref[:, cols] = (et_col * rq) * q32 - result[128:, :128]
        lo_ref[:, cols] = result[128:, 128:]

    waiting, running, tick = [one_head(g) for g in heads], [], 0
    while waiting or running:
        if waiting and tick % SKEW == 0:
            running.extend(waiting[:ABREAST])
            waiting = waiting[ABREAST:]
        running = [work for work in running if next(work, work) is None]
        tick += 1


def local_part(query, keys, values, beta, gate_log, count):
    heads = gate_log.shape[0]
    wide = GROUP * 128
    whole = lambda shape: pl.BlockSpec(shape, lambda i: (0,) * len(shape))
    return pl.pallas_call(
        local_kernel,
        grid=(heads // GROUP,),
        in_specs=[
            pl.BlockSpec((TOK, wide), lambda i: (0, i)),
            pl.BlockSpec((TOK, NH, wide), lambda i: (0, 0, i)),
            pl.BlockSpec((TOK, NH, wide), lambda i: (0, 0, i)),
            whole(beta.shape),
            whole(gate_log.shape),
            whole(count.shape),
        ],
        out_specs=[
            pl.BlockSpec((GROUP, 128, 256), lambda i: (i, 0, 0)),
            pl.BlockSpec((TOK, wide), lambda i: (0, i)),
            pl.BlockSpec((TOK, wide), lambda i: (0, i)),
        ],
        out_shape=[
            jax.ShapeDtypeStruct((heads, 128, 256), bf16),
            jax.ShapeDtypeStruct((TOK, heads * 128), f32),
            jax.ShapeDtypeStruct((TOK, heads * 128), f32),
        ],
        name="local",
    )(query, keys, values, beta, gate_log, count)


def joined(later, earlier):
    f_high, f_low = split(later[:, :128])
    e_high, e_low = split(earlier)
    moved = dot(across(f_high, f_low), down(e_high, e_high)) + dot(f_high, e_low)
    return earlier + later - moved


def total_kernel(pieces_ref, total_ref, mult_ref, add_ref):
    level = [pieces_ref[c].astype(f32) for c in range(pieces_ref.shape[0])]
    kept = []
    while len(level) > 1:
        level = [joined(level[i + 1], level[i]) for i in range(0, len(level), 2)]
        kept = level[0::2] + kept
    total_ref[...] = kept[0].astype(bf16)
    for i, node in enumerate(kept[1:]):
        mult_ref[i] = across(*split(node[:, :128]))
        add_ref[i] = node[:, 128:]


def states_kernel(plane_ref, one_ref, two_ref, three_ref, pieces_ref, mult_ref, add_ref, out_ref):
    plane = plane_ref[0]
    state = jnp.where(plane > 2, three_ref[:, 128:].astype(f32), 0.0)

    def stepped(piece, state):
        factor = piece[:, :128]
        high, low = split(state)
        moved = dot(across(factor, factor), down(high, low))
        return state + piece[:, 128:].astype(f32) - moved

    for back, ref in ((2, two_ref), (1, one_ref)):
        state = jnp.where(plane >= back, stepped(ref[...], state), 0.0)
    starts, node = [state], 0
    while 2 * len(starts) < pieces_ref.shape[0]:
        finer = []
        for state in starts:
            high, low = split(state)
            mult = mult_ref[node]
            moved = dot(mult, down(high, high)) + dot(mult[:, :128], low)
            finer += [state, state + add_ref[node] - moved]
            node += 1
        starts = finer
    for i, state in enumerate(starts):
        out_ref[2 * i] = state.astype(bf16)
        out_ref[2 * i + 1] = stepped(pieces_ref[2 * i], state).astype(bf16)


def read_kernel(qe_ref, lo_ref, state_ref, gate_ref, gain_ref, out_ref):
    for g in range(state_ref.shape[0]):
        cols = slice(g * 128, (g + 1) * 128)
        high, low = split(qe_ref[:, cols])
        state = state_ref[g]
        out = lo_ref[:, cols] + dot(across(high, low), down(state, state))
        inverse_rms = lax.rsqrt(jnp.mean(out * out, axis=1, keepdims=True) + epsilon)
        gate = gate_ref[:, cols].astype(f32)
        silu = gate / (1.0 + jnp.exp(-gate))
        out_ref[:, cols] = (out * inverse_rms * gain_ref[...] * silu).astype(bf16)


def read_part(query_eff, local_out, states, out_gate, norm_gain):
    heads = states.shape[0]
    wide = GROUP * 128
    block = pl.BlockSpec((TOK, wide), lambda i: (0, i))
    return pl.pallas_call(
        read_kernel,
        grid=(heads // GROUP,),
        in_specs=[
            block,
            block,
            pl.BlockSpec((GROUP, 128, 128), lambda i: (i, 0, 0)),
            block,
            pl.BlockSpec((1, 128), lambda i: (0, 0)),
        ],
        out_specs=block,
        out_shape=jax.ShapeDtypeStruct(query_eff.shape, bf16),
        compiler_params=pltpu.CompilerParams(vmem_limit_bytes=32 * MIB),
        name="read",
    )(*map(in_hbm, (query_eff, local_out, states, out_gate, norm_gain.reshape(1, DV))))


def own_kernel(half_ref, rows_ref, weight_ref, out_ref):
    out_ref[...] = dot(rows_ref[...], weight_ref[...])


def other_kernel(half_ref, rows_ref, weight_ref, first_ref, out_ref):
    out_ref[...] = (first_ref[...] + dot(rows_ref[...], weight_ref[...])).astype(bf16)


def half_projection(half, rows, weight, first=None):
    depth, columns = rows.shape[1], weight.shape[1]
    wide = 1024
    block = pl.BlockSpec((TOK, wide), lambda i, half: (0, i))
    specs = [
        pl.BlockSpec((TOK, depth), lambda i, half: (0, 0)),
        pl.BlockSpec((depth, wide), lambda i, half: (half[0], i)),
    ]
    args = [half, rows, in_hbm(weight)]
    if first is not None:
        specs.append(block)
        args.append(first)
    return pl.pallas_call(
        own_kernel if first is None else other_kernel,
        grid_spec=pltpu.PrefetchScalarGridSpec(
            num_scalar_prefetch=1, grid=(columns // wide,), in_specs=specs, out_specs=block
        ),
        out_shape=jax.ShapeDtypeStruct((TOK, columns), f32 if first is None else bf16),
        cost_estimate=pl.CostEstimate(
            flops=2 * TOK * depth * columns, bytes_accessed=2 * depth * columns, transcendentals=0
        ),
        compiler_params=pltpu.CompilerParams(vmem_limit_bytes=32 * MIB),
        name="own_half" if first is None else "other_half",
    )(*args)


def shards(query, keys, values, beta, gate_log, house_count, out_gate, norm_gain, out_weight):
    heads = query.shape[1] // DK
    pieces, query_eff, local_out = local_part(
        query,
        keys,
        values,
        beta,
        gate_log,
        house_count.reshape(1, TOK),
    )
    mine = lax.all_to_all(pieces, PLANE, 0, 0, tiled=True)
    chunks = mine.shape[0]
    nodes = chunks // 2 - 1
    total, mult, add = pl.pallas_call(
        total_kernel,
        out_shape=[
            jax.ShapeDtypeStruct((128, 256), bf16),
            jax.ShapeDtypeStruct((nodes, 128, 256), bf16),
            jax.ShapeDtypeStruct((nodes, 128, 128), f32),
        ],
        compiler_params=pltpu.CompilerParams(vmem_limit_bytes=32 * MIB),
        name="total",
    )(in_hbm(mine))
    planes = lax.axis_size("seq_0")
    before = [
        lax.ppermute(total, "seq_0", [(a, (a + s) % planes) for a in range(planes)])
        for s in range(1, planes)
    ]
    plane = lax.axis_index("seq_0").reshape(1).astype(jnp.int32)
    states = pl.pallas_call(
        states_kernel,
        in_specs=[pl.BlockSpec(memory_space=pltpu.SMEM)] + [pl.BlockSpec()] * 6,
        out_shape=jax.ShapeDtypeStruct((chunks, 128, 128), bf16),
        compiler_params=pltpu.CompilerParams(vmem_limit_bytes=32 * MIB),
        name="states",
    )(plane, *before, in_hbm(mine), mult, add)
    states = lax.all_to_all(states, PLANE, 0, 0, tiled=True)
    gated = read_part(query_eff, local_out, states, out_gate, norm_gain)
    other = lax.ppermute(gated, "head", [(0, 1), (1, 0)])
    half = lax.axis_index("head").reshape(1).astype(jnp.int32)
    partial = half_projection(half, gated, out_weight)
    return half_projection(1 - half, other, out_weight, partial)


def solution(mesh):
    finer = Mesh(
        mesh.devices.reshape(4, 4, 4, mesh.shape["head"]), ("seq_0", "seq_1", "seq_2", "head")
    )
    in_specs = (
        P(SEQ, "head"),
        P(SEQ, None, "head"),
        P(SEQ, None, "head"),
        P(None, "head", SEQ),
        P("head", SEQ),
        P(SEQ),
        P(SEQ, "head"),
        P(),
        P(None, "head"),
    )
    out_specs = P(SEQ, "head")
    return jax.shard_map(
        shards, mesh=finer, in_specs=in_specs, out_specs=out_specs, check_vma=False
    )
```

```python
import functools

import jax
import jax.numpy as jnp
from jax import lax
from jax.experimental import pallas as pl
from jax.experimental.pallas import tpu as pltpu
from jax.sharding import Mesh
from jax.sharding import PartitionSpec as P

DK = 128
DV = 128
NH = 2
TOK = 128
STEPS = TOK * NH
SEQ = ("seq_0", "seq_1", "seq_2")
PLANE = ("seq_1", "seq_2")
GROUP = 8
ARRIVE = (0, 4, 16)
LEAVE = (0, 8, 13, 16)
SKEW = 1
ABREAST = 1
MIB = 1024 * 1024
epsilon = 1e-06
f32, bf16 = jnp.float32, jnp.bfloat16


def dot(a, b):
    return jnp.dot(a, b, preferred_element_type=f32)


def dot_nt(a, b):
    return lax.dot_general(a, b, (((1,), (1,)), ((), ())), preferred_element_type=f32)


def split(x):
    high = x.astype(bf16)
    return high, (x - high.astype(f32)).astype(bf16)


def across(a, b):
    return jnp.concatenate([a, b], axis=1)


def down(a, b):
    return jnp.concatenate([a, b], axis=0)


def paired(a, b):
    zero = jnp.zeros_like(a)
    return down(across(a, zero), across(zero, b))


def pieces_product(a, b):
    (a_high, a_low), (b_high, b_low) = a, b
    return dot(across(a_high, a_low), down(b_high, b_high)) + dot(a_high, b_low)


def in_hbm(x):
    return pltpu.with_memory_space_constraint(x, pltpu.HBM)


def iota(shape, dim):
    return lax.broadcasted_iota(jnp.int32, shape, dim)


def local_kernel(
    q_hbm, k_hbm, v_hbm, beta_ref, gate_ref, count_ref, send_hbm, qe_hbm, lo_hbm,
    q_ref, k_ref, v_ref, send_ref, qe_ref, lo_ref, in_sems, out_sems,
):
    count_heads = gate_ref.shape[0]
    heads = range(count_heads)

    def fetch(batch):
        first, last = ARRIVE[batch], ARRIVE[batch + 1]
        cols = pl.ds(first * 128, (last - first) * 128)
        return [
            pltpu.make_async_copy(k_hbm.at[:, :, cols], k_ref.at[:, :, cols], in_sems.at[0, batch]),
            pltpu.make_async_copy(v_hbm.at[:, :, cols], v_ref.at[:, :, cols], in_sems.at[1, batch]),
            pltpu.make_async_copy(q_hbm.at[:, cols], q_ref.at[:, cols], in_sems.at[2, batch]),
        ]

    def put(batch):
        first, last = LEAVE[batch], LEAVE[batch + 1]
        rows, cols = pl.ds(first, last - first), pl.ds(first * 128, (last - first) * 128)
        return [
            pltpu.make_async_copy(send_ref.at[rows], send_hbm.at[rows], out_sems.at[0, batch]),
            pltpu.make_async_copy(qe_ref.at[:, cols], qe_hbm.at[:, cols], out_sems.at[1, batch]),
            pltpu.make_async_copy(lo_ref.at[:, cols], lo_hbm.at[:, cols], out_sems.at[2, batch]),
        ]

    for batch in range(len(ARRIVE) - 1):
        for copy in fetch(batch):
            copy.start()
    token, step = iota((TOK, STEPS), 0), iota((TOK, STEPS), 1)
    highest = lax.Precision.HIGHEST

    def place(rows, chosen):
        return jnp.dot(rows, chosen.astype(f32), precision=highest, preferred_element_type=f32)

    gates = gate_ref[...]
    count = count_ref[...]
    cum = place(gates, token * NH <= step)
    cum_tok = place(gates, iota((TOK, TOK), 0) <= iota((TOK, TOK), 1))
    strength = sum(
        place(jnp.where(j < count, beta_ref[j], 0.0), step == token * NH + j)
        for j in range(NH)
    )
    end = cum[:, STEPS - 1 :]
    stacked = jnp.concatenate(
        [
            cum,
            strength,
            strength * jnp.exp(cum),
            jnp.exp(end - cum),
            jnp.zeros((128 - 4 * count_heads, STEPS), f32),
        ],
        axis=0,
    )
    columns = down(stacked[:, :128].T, stacked[:, 128:].T)
    tok_columns = jnp.concatenate(
        [cum_tok, jnp.exp(cum_tok), jnp.zeros((128 - 2 * count_heads, TOK), f32)], axis=0
    ).T

    row, lane = iota((128, 128), 0), iota((128, 128), 1)
    eye = row == lane
    strictly = row > lane
    lane16 = iota((16, 128), 1)
    group16 = lane16 // 16
    eye16 = jnp.where(iota((16, 128), 0) == lane16 % 16, 1.0, 0.0).astype(f32)
    visible = step <= token * NH + (NH - 1)

    ones = jnp.where(eye, 1.0, 0.0)
    levels = []
    for size in (16, 32, 64):
        odd = (row // (2 * size) == lane // (2 * size)) & ((row // size) % 2 == 1)
        levels.append(jnp.where(odd & ((lane // size) % 2 == 0), 1.0, 0.0).astype(bf16))
    spread_from = [group16[:8] * 16 + r for r in range(15)]

    def one_head(g):
        if g in ARRIVE:
            for copy in fetch(ARRIVE.index(g)):
                copy.wait()
        cols = slice(g * 128, (g + 1) * 128)
        q = q_ref[:, cols]
        k, v = (ref[:, :, cols].reshape(STEPS, 128) for ref in (k_ref, v_ref))
        q32, k32, v32 = q.astype(f32), k.astype(f32), v.astype(f32)
        gram = dot_nt(k, k)
        scores = dot_nt(q, k)
        rk = lax.rsqrt(jnp.sum(k32 * k32, axis=1, keepdims=True) + epsilon)
        rq = lax.rsqrt(jnp.sum(q32 * q32, axis=1, keepdims=True) + epsilon)
        yield
        squares = [
            jnp.sum(jnp.where(eye, gram[a : a + 128, a : a + 128], 0.0), axis=0, keepdims=True)
            for a in (0, 128)
        ]
        rk_row = lax.rsqrt(across(*squares) + epsilon)
        c_row = cum[g : g + 1, :]
        c_col = columns[:, g : g + 1]
        b_col = columns[:, count_heads + g : count_heads + g + 1]
        be_col = columns[:, 2 * count_heads + g : 2 * count_heads + g + 1]
        f_col = columns[:, 3 * count_heads + g : 3 * count_heads + g + 1]
        ct_col = tok_columns[:, g : g + 1]
        et_col = tok_columns[:, count_heads + g : count_heads + g + 1]
        scale = b_col * rk

        def weighted(i, j):
            return (
                jnp.exp(c_col[i : i + 128] - c_row[:, j : j + 128])
                * gram[i : i + 128, j : j + 128]
                * scale[i : i + 128]
                * rk_row[:, j : j + 128]
            )

        lower = [jnp.where(strictly, weighted(a, a), 0.0) for a in (0, 128)]
        yield
        solved, compact = [eye16, eye16], []
        for part in lower:
            picked = part[:16]
            for b in range(1, 8):
                picked = jnp.where(group16 == b, part[16 * b : 16 * b + 16], picked)
            compact.append(picked)
        solved, compact = [[x[:8], x[8:]] for x in solved], [[x[:8], x[8:]] for x in compact]
        for r in range(15):
            for i in range(2):
                source = solved[i][r // 8][r % 8 : r % 8 + 1]
                for part in range((r + 1) // 8, 2):
                    spread = jnp.take_along_axis(compact[i][part], spread_from[r], axis=1)
                    solved[i][part] = solved[i][part] - spread * source
            if r % 5 == 4:
                yield
        one, two = [
            jnp.concatenate([jnp.where(group16 == b, down(*x), 0.0) for b in range(8)], axis=0)
            for x in solved
        ]
        low = [split(part) for part in lower]
        for odd in levels:
            picked = across(low[0][0] * odd, low[1][0] * odd)
            narrow = one.astype(bf16), two.astype(bf16)
            mid = dot(picked, paired(*narrow)).astype(bf16)
            yield
            out = dot(across(*narrow), paired(mid[:, :128], mid[:, 128:]))
            one, two = one - out[:, :128], two - out[:, 128:]
            yield
        rounded = one.astype(bf16), two.astype(bf16)
        pair = paired(*rounded)
        near = dot(across(low[0][0], low[1][0]), pair) + dot(across(low[0][1], low[1][1]), pair)
        rest = [
            (ones - part.astype(f32) - near[:, a : a + 128]).astype(bf16)
            for part, a in zip(rounded, (0, 128))
        ]
        yield
        out = dot(across(*rounded), paired(*rest)).astype(bf16)
        one, two = (rounded[0], out[:, :128]), (rounded[1], out[:, 128:])
        yield
        right = across((be_col * rk) * k32, b_col * v32)
        top = pieces_product(one, split(right[:128]))
        yield
        rest = right[128:] - pieces_product(split(weighted(128, 0)), split(top))
        yield
        bottom = pieces_product(two, split(rest))
        faded = (f_col * rk) * k32
        yield
        reads = jnp.where(visible, jnp.exp(ct_col - c_row) * scores * rq * rk_row, 0.0)
        x_high, x_low = split(down(top, bottom))
        p_high, p_low = split(down(across(faded[:128].T, faded[128:].T), reads))
        result = dot(p_high, x_high) + dot(p_low, x_high) + dot(p_high, x_low)
        yield
        lost = 1.0 - jnp.exp(end[g : g + 1])
        send_ref[g] = across(
            result[:128, :128] + jnp.where(eye, lost, 0.0), result[:128, 128:]
        ).astype(bf16)
        qe_ref[:, cols] = (et_col * rq) * q32 - result[128:, :128]
        lo_ref[:, cols] = result[128:, 128:]
        if g + 1 in LEAVE:
            for copy in put(LEAVE.index(g + 1) - 1):
                copy.start()

    waiting, running, tick = [one_head(g) for g in heads], [], 0
    while waiting or running:
        if waiting and tick % SKEW == 0:
            running.extend(waiting[:ABREAST])
            waiting = waiting[ABREAST:]
        running = [work for work in running if next(work, work) is None]
        tick += 1
    for batch in range(len(LEAVE) - 1):
        for copy in put(batch):
            copy.wait()


def local_part(query, keys, values, beta, gate_log, count):
    heads = gate_log.shape[0]
    anywhere = pl.BlockSpec(memory_space=pl.ANY)
    shapes = [((heads, 128, 256), bf16), (query.shape, f32), (query.shape, f32)]
    return pl.pallas_call(
        local_kernel,
        in_specs=[anywhere] * 3 + [pl.BlockSpec()] * 3,
        out_specs=[anywhere] * 3,
        out_shape=[jax.ShapeDtypeStruct(*shape) for shape in shapes],
        scratch_shapes=[
            *[pltpu.VMEM(x.shape, x.dtype) for x in (query, keys, values)],
            *[pltpu.VMEM(*shape) for shape in shapes],
            pltpu.SemaphoreType.DMA((3, len(ARRIVE) - 1)),
            pltpu.SemaphoreType.DMA((3, len(LEAVE) - 1)),
        ],
        name="local",
    )(query, keys, values, beta, gate_log, count)


def joined(later, earlier):
    f_high, f_low = split(later[:, :128])
    e_high, e_low = split(earlier)
    moved = dot(across(f_high, f_low), down(e_high, e_high)) + dot(f_high, e_low)
    return earlier + later - moved


def total_kernel(pieces_ref, total_ref, mult_ref, add_ref):
    level = [pieces_ref[c].astype(f32) for c in range(pieces_ref.shape[0])]
    kept = []
    while len(level) > 1:
        level = [joined(level[i + 1], level[i]) for i in range(0, len(level), 2)]
        kept = level[0::2] + kept
    total_ref[...] = kept[0].astype(bf16)
    for i, node in enumerate(kept[1:]):
        mult_ref[i] = across(*split(node[:, :128]))
        add_ref[i] = node[:, 128:]


def states_kernel(plane_ref, one_ref, two_ref, three_ref, pieces_ref, mult_ref, add_ref, out_ref):
    plane = plane_ref[0]
    state = jnp.where(plane > 2, three_ref[:, 128:].astype(f32), 0.0)

    def stepped(piece, state):
        factor = piece[:, :128]
        high, low = split(state)
        moved = dot(across(factor, factor), down(high, low))
        return state + piece[:, 128:].astype(f32) - moved

    for back, ref in ((2, two_ref), (1, one_ref)):
        state = jnp.where(plane >= back, stepped(ref[...], state), 0.0)
    starts, node = [state], 0
    while 2 * len(starts) < pieces_ref.shape[0]:
        finer = []
        for state in starts:
            high, low = split(state)
            mult = mult_ref[node]
            moved = dot(mult, down(high, high)) + dot(mult[:, :128], low)
            finer += [state, state + add_ref[node] - moved]
            node += 1
        starts = finer
    for i, state in enumerate(starts):
        out_ref[2 * i] = state.astype(bf16)
        out_ref[2 * i + 1] = stepped(pieces_ref[2 * i], state).astype(bf16)


def read_kernel(qe_ref, lo_ref, state_ref, gate_ref, gain_ref, out_ref):
    for g in range(state_ref.shape[0]):
        cols = slice(g * 128, (g + 1) * 128)
        high, low = split(qe_ref[:, cols])
        state = state_ref[g]
        out = lo_ref[:, cols] + dot(across(high, low), down(state, state))
        inverse_rms = lax.rsqrt(jnp.mean(out * out, axis=1, keepdims=True) + epsilon)
        gate = gate_ref[:, cols].astype(f32)
        silu = gate / (1.0 + jnp.exp(-gate))
        out_ref[:, cols] = (out * inverse_rms * gain_ref[...] * silu).astype(bf16)


def read_part(query_eff, local_out, states, out_gate, norm_gain):
    heads = states.shape[0]
    wide = GROUP * 128
    block = pl.BlockSpec((TOK, wide), lambda i: (0, i))
    return pl.pallas_call(
        read_kernel,
        grid=(heads // GROUP,),
        in_specs=[
            block,
            block,
            pl.BlockSpec((GROUP, 128, 128), lambda i: (i, 0, 0)),
            block,
            pl.BlockSpec((1, 128), lambda i: (0, 0)),
        ],
        out_specs=block,
        out_shape=jax.ShapeDtypeStruct(query_eff.shape, bf16),
        compiler_params=pltpu.CompilerParams(vmem_limit_bytes=32 * MIB),
        name="read",
    )(*map(in_hbm, (query_eff, local_out, states, out_gate, norm_gain.reshape(1, DV))))


def own_kernel(half_ref, rows_ref, weight_ref, out_ref):
    out_ref[...] = dot(rows_ref[...], weight_ref[...])


def other_kernel(half_ref, rows_ref, weight_ref, first_ref, out_ref):
    out_ref[...] = (first_ref[...] + dot(rows_ref[...], weight_ref[...])).astype(bf16)


def half_projection(half, rows, weight, first=None):
    depth, columns = rows.shape[1], weight.shape[1]
    wide = 1024
    block = pl.BlockSpec((TOK, wide), lambda i, half: (0, i))
    specs = [
        pl.BlockSpec((TOK, depth), lambda i, half: (0, 0)),
        pl.BlockSpec((depth, wide), lambda i, half: (half[0], i)),
    ]
    args = [half, rows, in_hbm(weight)]
    if first is not None:
        specs.append(block)
        args.append(first)
    return pl.pallas_call(
        own_kernel if first is None else other_kernel,
        grid_spec=pltpu.PrefetchScalarGridSpec(
            num_scalar_prefetch=1, grid=(columns // wide,), in_specs=specs, out_specs=block
        ),
        out_shape=jax.ShapeDtypeStruct((TOK, columns), f32 if first is None else bf16),
        cost_estimate=pl.CostEstimate(
            flops=2 * TOK * depth * columns, bytes_accessed=2 * depth * columns, transcendentals=0
        ),
        compiler_params=pltpu.CompilerParams(vmem_limit_bytes=32 * MIB),
        name="own_half" if first is None else "other_half",
    )(*args)


def shards(query, keys, values, beta, gate_log, house_count, out_gate, norm_gain, out_weight):
    heads = query.shape[1] // DK
    pieces, query_eff, local_out = local_part(
        query,
        keys,
        values,
        beta,
        gate_log,
        house_count.reshape(1, TOK),
    )
    mine = lax.all_to_all(pieces, PLANE, 0, 0, tiled=True)
    chunks = mine.shape[0]
    nodes = chunks // 2 - 1
    total, mult, add = pl.pallas_call(
        total_kernel,
        out_shape=[
            jax.ShapeDtypeStruct((128, 256), bf16),
            jax.ShapeDtypeStruct((nodes, 128, 256), bf16),
            jax.ShapeDtypeStruct((nodes, 128, 128), f32),
        ],
        compiler_params=pltpu.CompilerParams(vmem_limit_bytes=32 * MIB),
        name="total",
    )(in_hbm(mine))
    planes = lax.axis_size("seq_0")
    before = [
        lax.ppermute(total, "seq_0", [(a, (a + s) % planes) for a in range(planes)])
        for s in range(1, planes)
    ]
    plane = lax.axis_index("seq_0").reshape(1).astype(jnp.int32)
    states = pl.pallas_call(
        states_kernel,
        in_specs=[pl.BlockSpec(memory_space=pltpu.SMEM)] + [pl.BlockSpec()] * 6,
        out_shape=jax.ShapeDtypeStruct((chunks, 128, 128), bf16),
        compiler_params=pltpu.CompilerParams(vmem_limit_bytes=32 * MIB),
        name="states",
    )(plane, *before, in_hbm(mine), mult, add)
    states = lax.all_to_all(states, PLANE, 0, 0, tiled=True)
    gated = read_part(query_eff, local_out, states, out_gate, norm_gain)
    other = lax.ppermute(gated, "head", [(0, 1), (1, 0)])
    half = lax.axis_index("head").reshape(1).astype(jnp.int32)
    partial = half_projection(half, gated, out_weight)
    return half_projection(1 - half, other, out_weight, partial)


def solution(mesh):
    finer = Mesh(
        mesh.devices.reshape(4, 4, 4, mesh.shape["head"]), ("seq_0", "seq_1", "seq_2", "head")
    )
    in_specs = (
        P(SEQ, "head"),
        P(SEQ, None, "head"),
        P(SEQ, None, "head"),
        P(None, "head", SEQ),
        P("head", SEQ),
        P(SEQ),
        P(SEQ, "head"),
        P(),
        P(None, "head"),
    )
    out_specs = P(SEQ, "head")
    return jax.shard_map(
        shards, mesh=finer, in_specs=in_specs, out_specs=out_specs, check_vma=False
    )
```

```python
import functools

import jax
import jax.numpy as jnp
from jax import lax
from jax.experimental import pallas as pl
from jax.experimental.pallas import tpu as pltpu
from jax.sharding import Mesh
from jax.sharding import PartitionSpec as P

DK = 128
DV = 128
NH = 2
TOK = 128
STEPS = TOK * NH
SEQ = ("seq_0", "seq_1", "seq_2")
PLANE = ("seq_1", "seq_2")
GROUP = 8
ARRIVE = (0, 4, 16)
LEAVE = (0, 8, 13, 16)
SKEW = 1
ABREAST = 1
MIB = 1024 * 1024
epsilon = 1e-06
f32, bf16 = jnp.float32, jnp.bfloat16


def dot(a, b):
    return jnp.dot(a, b, preferred_element_type=f32)


def dot_nt(a, b):
    return lax.dot_general(a, b, (((1,), (1,)), ((), ())), preferred_element_type=f32)


def split(x):
    high = x.astype(bf16)
    return high, (x - high.astype(f32)).astype(bf16)


def across(a, b):
    return jnp.concatenate([a, b], axis=1)


def down(a, b):
    return jnp.concatenate([a, b], axis=0)


def paired(a, b):
    zero = jnp.zeros_like(a)
    return down(across(a, zero), across(zero, b))


def pieces_product(a, b):
    (a_high, a_low), (b_high, b_low) = a, b
    return dot(across(a_high, a_low), down(b_high, b_high)) + dot(a_high, b_low)


def in_hbm(x):
    return pltpu.with_memory_space_constraint(x, pltpu.HBM)


def iota(shape, dim):
    return lax.broadcasted_iota(jnp.int32, shape, dim)


def local_kernel(
    q_hbm, k_hbm, v_hbm, beta_ref, gate_ref, count_ref, send_hbm, qe_hbm, lo_hbm,
    q_ref, k_ref, v_ref, send_ref, qe_ref, lo_ref, in_sems, out_sems,
):
    count_heads = gate_ref.shape[0]
    heads = range(count_heads)

    def fetch(batch):
        first, last = ARRIVE[batch], ARRIVE[batch + 1]
        cols = pl.ds(first * 128, (last - first) * 128)
        return [
            pltpu.make_async_copy(k_hbm.at[:, :, cols], k_ref.at[:, :, cols], in_sems.at[0, batch]),
            pltpu.make_async_copy(v_hbm.at[:, :, cols], v_ref.at[:, :, cols], in_sems.at[1, batch]),
            pltpu.make_async_copy(q_hbm.at[:, cols], q_ref.at[:, cols], in_sems.at[2, batch]),
        ]

    def put(batch):
        first, last = LEAVE[batch], LEAVE[batch + 1]
        rows, cols = pl.ds(first, last - first), pl.ds(first * 128, (last - first) * 128)
        return [
            pltpu.make_async_copy(send_ref.at[rows], send_hbm.at[rows], out_sems.at[0, batch]),
            pltpu.make_async_copy(qe_ref.at[:, cols], qe_hbm.at[:, cols], out_sems.at[1, batch]),
            pltpu.make_async_copy(lo_ref.at[:, cols], lo_hbm.at[:, cols], out_sems.at[2, batch]),
        ]

    for batch in range(len(ARRIVE) - 1):
        for copy in fetch(batch):
            copy.start()
    token, step = iota((TOK, STEPS), 0), iota((TOK, STEPS), 1)
    highest = lax.Precision.HIGHEST

    def place(rows, chosen):
        return jnp.dot(rows, chosen.astype(f32), precision=highest, preferred_element_type=f32)

    gates = gate_ref[...]
    count = count_ref[...]
    cum = place(gates, token * NH <= step)
    cum_tok = place(gates, iota((TOK, TOK), 0) <= iota((TOK, TOK), 1))
    strength = sum(
        place(jnp.where(j < count, beta_ref[j], 0.0), step == token * NH + j)
        for j in range(NH)
    )
    end = cum[:, STEPS - 1 :]
    stacked = jnp.concatenate(
        [
            cum,
            strength,
            strength * jnp.exp(cum),
            jnp.exp(end - cum),
            jnp.zeros((128 - 4 * count_heads, STEPS), f32),
        ],
        axis=0,
    )
    columns = down(stacked[:, :128].T, stacked[:, 128:].T)
    tok_columns = jnp.concatenate(
        [cum_tok, jnp.exp(cum_tok), jnp.zeros((128 - 2 * count_heads, TOK), f32)], axis=0
    ).T

    row, lane = iota((128, 128), 0), iota((128, 128), 1)
    eye = row == lane
    strictly = row > lane
    lane16 = iota((16, 128), 1)
    group16 = lane16 // 16
    eye16 = jnp.where(iota((16, 128), 0) == lane16 % 16, 1.0, 0.0).astype(f32)
    visible = step <= token * NH + (NH - 1)

    ones = jnp.where(eye, 1.0, 0.0)
    levels = []
    for size in (16, 32, 64):
        odd = (row // (2 * size) == lane // (2 * size)) & ((row // size) % 2 == 1)
        levels.append(jnp.where(odd & ((lane // size) % 2 == 0), 1.0, 0.0).astype(bf16))
    spread_from = [group16[:8] * 16 + r for r in range(15)]

    def one_head(g):
        if g in ARRIVE:
            for copy in fetch(ARRIVE.index(g)):
                copy.wait()
        cols = slice(g * 128, (g + 1) * 128)
        q = q_ref[:, cols]
        k, v = (ref[:, :, cols].reshape(STEPS, 128) for ref in (k_ref, v_ref))
        q32, k32, v32 = q.astype(f32), k.astype(f32), v.astype(f32)
        gram = dot_nt(k, k)
        scores = dot_nt(q, k)
        rk = lax.rsqrt(jnp.sum(k32 * k32, axis=1, keepdims=True) + epsilon)
        rq = lax.rsqrt(jnp.sum(q32 * q32, axis=1, keepdims=True) + epsilon)
        yield
        squares = [
            jnp.sum(jnp.where(eye, gram[a : a + 128, a : a + 128], 0.0), axis=0, keepdims=True)
            for a in (0, 128)
        ]
        rk_row = lax.rsqrt(across(*squares) + epsilon)
        c_row = cum[g : g + 1, :]
        c_col = columns[:, g : g + 1]
        b_col = columns[:, count_heads + g : count_heads + g + 1]
        be_col = columns[:, 2 * count_heads + g : 2 * count_heads + g + 1]
        f_col = columns[:, 3 * count_heads + g : 3 * count_heads + g + 1]
        ct_col = tok_columns[:, g : g + 1]
        et_col = tok_columns[:, count_heads + g : count_heads + g + 1]
        scale = b_col * rk

        def weighted(i, j):
            return (
                jnp.exp(c_col[i : i + 128] - c_row[:, j : j + 128])
                * gram[i : i + 128, j : j + 128]
                * scale[i : i + 128]
                * rk_row[:, j : j + 128]
            )

        lower = [jnp.where(strictly, weighted(a, a), 0.0) for a in (0, 128)]
        yield
        solved, compact = [eye16, eye16], []
        for part in lower:
            picked = part[:16]
            for b in range(1, 8):
                picked = jnp.where(group16 == b, part[16 * b : 16 * b + 16], picked)
            compact.append(picked)
        solved, compact = [[x[:8], x[8:]] for x in solved], [[x[:8], x[8:]] for x in compact]
        for r in range(15):
            for i in range(2):
                source = solved[i][r // 8][r % 8 : r % 8 + 1]
                for part in range((r + 1) // 8, 2):
                    spread = jnp.take_along_axis(compact[i][part], spread_from[r], axis=1)
                    solved[i][part] = solved[i][part] - spread * source
            if r % 5 == 4:
                yield
        one, two = [
            jnp.concatenate([jnp.where(group16 == b, down(*x), 0.0) for b in range(8)], axis=0)
            for x in solved
        ]
        low = [split(part) for part in lower]
        for odd in levels:
            picked = across(low[0][0] * odd, low[1][0] * odd)
            narrow = one.astype(bf16), two.astype(bf16)
            mid = dot(picked, paired(*narrow)).astype(bf16)
            yield
            out = dot(across(*narrow), paired(mid[:, :128], mid[:, 128:]))
            one, two = one - out[:, :128], two - out[:, 128:]
            yield
        rounded = one.astype(bf16), two.astype(bf16)
        pair = paired(*rounded)
        near = dot(across(low[0][0], low[1][0]), pair) + dot(across(low[0][1], low[1][1]), pair)
        rest = [
            (ones - part.astype(f32) - near[:, a : a + 128]).astype(bf16)
            for part, a in zip(rounded, (0, 128))
        ]
        yield
        out = dot(across(*rounded), paired(*rest)).astype(bf16)
        one, two = (rounded[0], out[:, :128]), (rounded[1], out[:, 128:])
        yield
        right = across((be_col * rk) * k32, b_col * v32)
        top = pieces_product(one, split(right[:128]))
        yield
        rest = right[128:] - pieces_product(split(weighted(128, 0)), split(top))
        yield
        bottom = pieces_product(two, split(rest))
        faded = (f_col * rk) * k32
        yield
        reads = jnp.where(visible, jnp.exp(ct_col - c_row) * scores * rq * rk_row, 0.0)
        x_high, x_low = split(down(top, bottom))
        p_high, p_low = split(down(across(faded[:128].T, faded[128:].T), reads))
        result = dot(p_high, x_high) + dot(p_low, x_high) + dot(p_high, x_low)
        yield
        lost = 1.0 - jnp.exp(end[g : g + 1])
        send_ref[g] = across(
            result[:128, :128] + jnp.where(eye, lost, 0.0), result[:128, 128:]
        ).astype(bf16)
        qe_ref[:, cols] = (et_col * rq) * q32 - result[128:, :128]
        lo_ref[:, cols] = result[128:, 128:]
        if g + 1 in LEAVE:
            for copy in put(LEAVE.index(g + 1) - 1):
                copy.start()

    waiting, running, tick = [one_head(g) for g in heads], [], 0
    while waiting or running:
        if waiting and tick % SKEW == 0:
            running.extend(waiting[:ABREAST])
            waiting = waiting[ABREAST:]
        running = [work for work in running if next(work, work) is None]
        tick += 1
    for batch in range(len(LEAVE) - 1):
        for copy in put(batch):
            copy.wait()


def local_part(query, keys, values, beta, gate_log, count):
    heads = gate_log.shape[0]
    anywhere = pl.BlockSpec(memory_space=pl.ANY)
    shapes = [((heads, 128, 256), bf16), (query.shape, f32), (query.shape, f32)]
    return pl.pallas_call(
        local_kernel,
        in_specs=[anywhere] * 3 + [pl.BlockSpec()] * 3,
        out_specs=[anywhere] * 3,
        out_shape=[jax.ShapeDtypeStruct(*shape) for shape in shapes],
        scratch_shapes=[
            *[pltpu.VMEM(x.shape, x.dtype) for x in (query, keys, values)],
            *[pltpu.VMEM(*shape) for shape in shapes],
            pltpu.SemaphoreType.DMA((3, len(ARRIVE) - 1)),
            pltpu.SemaphoreType.DMA((3, len(LEAVE) - 1)),
        ],
        name="local",
    )(query, keys, values, beta, gate_log, count)


def joined(later, earlier):
    f_high, f_low = split(later[:, :128])
    e_high, e_low = split(earlier)
    moved = dot(across(f_high, f_low), down(e_high, e_high)) + dot(f_high, e_low)
    return earlier + later - moved


def total_kernel(pieces_hbm, total_ref, mult_ref, add_ref, even_ref, pieces_ref, sems):
    chunks = pieces_hbm.shape[0]
    part = chunks // 2
    copies = [
        pltpu.make_async_copy(pieces_hbm.at[rows], pieces_ref.at[rows], sems.at[i])
        for i, rows in enumerate((pl.ds(0, part), pl.ds(part, part)))
    ]
    for copy in copies:
        copy.start()
    level, kept = [], []
    for c in range(0, chunks, 2):
        if c % part == 0:
            copies[c // part].wait()
        earlier, later = pieces_ref[c], pieces_ref[c + 1]
        even_ref[c // 2] = earlier
        level.append(earlier.astype(f32) + later.astype(f32) - dot(later[:, :128], earlier))
    kept = level[0::2]
    while len(level) > 1:
        level = [joined(level[i + 1], level[i]) for i in range(0, len(level), 2)]
        kept = level[0::2] + kept
    total_ref[...] = kept[0].astype(bf16)
    for i, node in enumerate(kept[1:]):
        mult_ref[i] = across(*split(node[:, :128]))
        add_ref[i] = node[:, 128:]


def states_kernel(plane_ref, one_ref, two_ref, three_ref, even_ref, mult_ref, add_ref, out_ref):
    plane = plane_ref[0]
    state = jnp.where(plane > 2, three_ref[:, 128:].astype(f32), 0.0)

    def stepped(piece, state):
        factor = piece[:, :128]
        high, low = split(state)
        moved = dot(across(factor, factor), down(high, low))
        return state + piece[:, 128:].astype(f32) - moved

    for back, ref in ((2, two_ref), (1, one_ref)):
        state = jnp.where(plane >= back, stepped(ref[...], state), 0.0)
    starts, node = [state], 0
    while len(starts) < even_ref.shape[0]:
        finer = []
        for state in starts:
            high, low = split(state)
            mult = mult_ref[node]
            moved = dot(mult, down(high, high)) + dot(mult[:, :128], low)
            finer += [state, state + add_ref[node] - moved]
            node += 1
        starts = finer
    for i, state in enumerate(starts):
        out_ref[2 * i] = state.astype(bf16)
        out_ref[2 * i + 1] = stepped(even_ref[i], state).astype(bf16)


def read_kernel(qe_ref, lo_ref, state_ref, gate_ref, gain_ref, out_ref):
    for g in range(state_ref.shape[0]):
        cols = slice(g * 128, (g + 1) * 128)
        high, low = split(qe_ref[:, cols])
        state = state_ref[g]
        out = lo_ref[:, cols] + dot(across(high, low), down(state, state))
        inverse_rms = lax.rsqrt(jnp.mean(out * out, axis=1, keepdims=True) + epsilon)
        gate = gate_ref[:, cols].astype(f32)
        silu = gate / (1.0 + jnp.exp(-gate))
        out_ref[:, cols] = (out * inverse_rms * gain_ref[...] * silu).astype(bf16)


def read_part(query_eff, local_out, states, out_gate, norm_gain):
    heads = states.shape[0]
    wide = GROUP * 128
    block = pl.BlockSpec((TOK, wide), lambda i: (0, i))
    return pl.pallas_call(
        read_kernel,
        grid=(heads // GROUP,),
        in_specs=[
            block,
            block,
            pl.BlockSpec((GROUP, 128, 128), lambda i: (i, 0, 0)),
            block,
            pl.BlockSpec((1, 128), lambda i: (0, 0)),
        ],
        out_specs=block,
        out_shape=jax.ShapeDtypeStruct(query_eff.shape, bf16),
        compiler_params=pltpu.CompilerParams(vmem_limit_bytes=32 * MIB),
        name="read",
    )(*map(in_hbm, (query_eff, local_out, states, out_gate, norm_gain.reshape(1, DV))))


def own_kernel(half_ref, rows_ref, weight_ref, out_ref):
    out_ref[...] = dot(rows_ref[...], weight_ref[...])


def other_kernel(half_ref, rows_ref, weight_ref, first_ref, out_ref):
    out_ref[...] = (first_ref[...] + dot(rows_ref[...], weight_ref[...])).astype(bf16)


def half_projection(half, rows, weight, first=None):
    depth, columns = rows.shape[1], weight.shape[1]
    wide = 1024
    block = pl.BlockSpec((TOK, wide), lambda i, half: (0, i))
    specs = [
        pl.BlockSpec((TOK, depth), lambda i, half: (0, 0)),
        pl.BlockSpec((depth, wide), lambda i, half: (half[0], i)),
    ]
    args = [half, rows, in_hbm(weight)]
    if first is not None:
        specs.append(block)
        args.append(first)
    return pl.pallas_call(
        own_kernel if first is None else other_kernel,
        grid_spec=pltpu.PrefetchScalarGridSpec(
            num_scalar_prefetch=1, grid=(columns // wide,), in_specs=specs, out_specs=block
        ),
        out_shape=jax.ShapeDtypeStruct((TOK, columns), f32 if first is None else bf16),
        cost_estimate=pl.CostEstimate(
            flops=2 * TOK * depth * columns, bytes_accessed=2 * depth * columns, transcendentals=0
        ),
        compiler_params=pltpu.CompilerParams(vmem_limit_bytes=32 * MIB),
        name="own_half" if first is None else "other_half",
    )(*args)


def shards(query, keys, values, beta, gate_log, house_count, out_gate, norm_gain, out_weight):
    heads = query.shape[1] // DK
    pieces, query_eff, local_out = local_part(
        query,
        keys,
        values,
        beta,
        gate_log,
        house_count.reshape(1, TOK),
    )
    mine = lax.all_to_all(pieces, PLANE, 0, 0, tiled=True)
    chunks = mine.shape[0]
    nodes = chunks // 2 - 1
    total, mult, add, even = pl.pallas_call(
        total_kernel,
        in_specs=[pl.BlockSpec(memory_space=pl.ANY)],
        out_shape=[
            jax.ShapeDtypeStruct((128, 256), bf16),
            jax.ShapeDtypeStruct((nodes, 128, 256), bf16),
            jax.ShapeDtypeStruct((nodes, 128, 128), f32),
            jax.ShapeDtypeStruct((chunks // 2, 128, 256), bf16),
        ],
        scratch_shapes=[pltpu.VMEM(mine.shape, bf16), pltpu.SemaphoreType.DMA((2,))],
        compiler_params=pltpu.CompilerParams(vmem_limit_bytes=32 * MIB),
        name="total",
    )(in_hbm(mine))
    planes = lax.axis_size("seq_0")
    before = [
        lax.ppermute(total, "seq_0", [(a, (a + s) % planes) for a in range(planes)])
        for s in range(planes - 1, 0, -1)
    ]
    plane = lax.axis_index("seq_0").reshape(1).astype(jnp.int32)
    states = pl.pallas_call(
        states_kernel,
        in_specs=[pl.BlockSpec(memory_space=pltpu.SMEM)] + [pl.BlockSpec()] * 6,
        out_shape=jax.ShapeDtypeStruct((chunks, 128, 128), bf16),
        compiler_params=pltpu.CompilerParams(vmem_limit_bytes=32 * MIB),
        name="states",
    )(plane, *before[::-1], even, mult, add)
    states = lax.all_to_all(states, PLANE, 0, 0, tiled=True)
    gated = read_part(query_eff, local_out, states, out_gate, norm_gain)
    other = lax.ppermute(gated, "head", [(0, 1), (1, 0)])
    half = lax.axis_index("head").reshape(1).astype(jnp.int32)
    partial = half_projection(half, gated, out_weight)
    return half_projection(1 - half, other, out_weight, partial)


def solution(mesh):
    finer = Mesh(
        mesh.devices.reshape(4, 4, 4, mesh.shape["head"]), ("seq_0", "seq_1", "seq_2", "head")
    )
    in_specs = (
        P(SEQ, "head"),
        P(SEQ, None, "head"),
        P(SEQ, None, "head"),
        P(None, "head", SEQ),
        P("head", SEQ),
        P(SEQ),
        P(SEQ, "head"),
        P(),
        P(None, "head"),
    )
    out_specs = P(SEQ, "head")
    return jax.shard_map(
        shards, mesh=finer, in_specs=in_specs, out_specs=out_specs, check_vma=False
    )
```

```python
import functools

import jax
import jax.numpy as jnp
from jax import lax
from jax.experimental import pallas as pl
from jax.experimental.pallas import tpu as pltpu
from jax.sharding import Mesh
from jax.sharding import PartitionSpec as P

DK = 128
DV = 128
NH = 2
TOK = 128
STEPS = TOK * NH
SEQ = ("seq_0", "seq_1", "seq_2")
PLANE = ("seq_1", "seq_2")
GROUP = 8
ARRIVE = (0, 4, 16)
LEAVE = (0, 8, 13, 16)
SKEW = 1
ABREAST = 1
MIB = 1024 * 1024
epsilon = 1e-06
f32, bf16 = jnp.float32, jnp.bfloat16


def dot(a, b):
    return jnp.dot(a, b, preferred_element_type=f32)


def dot_nt(a, b):
    return lax.dot_general(a, b, (((1,), (1,)), ((), ())), preferred_element_type=f32)


def split(x):
    high = x.astype(bf16)
    return high, (x - high.astype(f32)).astype(bf16)


def across(a, b):
    return jnp.concatenate([a, b], axis=1)


def down(a, b):
    return jnp.concatenate([a, b], axis=0)


def paired(a, b):
    zero = jnp.zeros_like(a)
    return down(across(a, zero), across(zero, b))


def pieces_product(a, b):
    (a_high, a_low), (b_high, b_low) = a, b
    return dot(across(a_high, a_low), down(b_high, b_high)) + dot(a_high, b_low)


def in_hbm(x):
    return pltpu.with_memory_space_constraint(x, pltpu.HBM)


def iota(shape, dim):
    return lax.broadcasted_iota(jnp.int32, shape, dim)


def local_kernel(
    q_hbm, k_hbm, v_hbm, beta_ref, gate_ref, count_ref, send_hbm, qe_hbm, lo_hbm,
    q_ref, k_ref, v_ref, send_ref, qe_ref, lo_ref, in_sems, out_sems,
):
    count_heads = gate_ref.shape[0]
    heads = range(count_heads)

    def fetch(batch):
        first, last = ARRIVE[batch], ARRIVE[batch + 1]
        cols = pl.ds(first * 128, (last - first) * 128)
        return [
            pltpu.make_async_copy(k_hbm.at[:, :, cols], k_ref.at[:, :, cols], in_sems.at[0, batch]),
            pltpu.make_async_copy(v_hbm.at[:, :, cols], v_ref.at[:, :, cols], in_sems.at[1, batch]),
            pltpu.make_async_copy(q_hbm.at[:, cols], q_ref.at[:, cols], in_sems.at[2, batch]),
        ]

    def put(batch):
        first, last = LEAVE[batch], LEAVE[batch + 1]
        rows, cols = pl.ds(first, last - first), pl.ds(first * 128, (last - first) * 128)
        return [
            pltpu.make_async_copy(send_ref.at[rows], send_hbm.at[rows], out_sems.at[0, batch]),
            pltpu.make_async_copy(qe_ref.at[:, cols], qe_hbm.at[:, cols], out_sems.at[1, batch]),
            pltpu.make_async_copy(lo_ref.at[:, cols], lo_hbm.at[:, cols], out_sems.at[2, batch]),
        ]

    for batch in range(len(ARRIVE) - 1):
        for copy in fetch(batch):
            copy.start()
    token, step = iota((TOK, STEPS), 0), iota((TOK, STEPS), 1)
    highest = lax.Precision.HIGHEST

    def place(rows, chosen):
        return jnp.dot(rows, chosen.astype(f32), precision=highest, preferred_element_type=f32)

    gates = gate_ref[...]
    count = count_ref[...]
    cum = place(gates, token * NH <= step)
    cum_tok = place(gates, iota((TOK, TOK), 0) <= iota((TOK, TOK), 1))
    strength = sum(
        place(jnp.where(j < count, beta_ref[j], 0.0), step == token * NH + j)
        for j in range(NH)
    )
    end = cum[:, STEPS - 1 :]
    stacked = jnp.concatenate(
        [
            cum,
            strength,
            strength * jnp.exp(cum),
            jnp.exp(end - cum),
            jnp.zeros((128 - 4 * count_heads, STEPS), f32),
        ],
        axis=0,
    )
    columns = down(stacked[:, :128].T, stacked[:, 128:].T)
    tok_columns = jnp.concatenate(
        [cum_tok, jnp.exp(cum_tok), jnp.zeros((128 - 2 * count_heads, TOK), f32)], axis=0
    ).T

    row, lane = iota((128, 128), 0), iota((128, 128), 1)
    eye = row == lane
    strictly = row > lane
    lane16 = iota((16, 128), 1)
    group16 = lane16 // 16
    eye16 = jnp.where(iota((16, 128), 0) == lane16 % 16, 1.0, 0.0).astype(f32)
    visible = step <= token * NH + (NH - 1)

    ones = jnp.where(eye, 1.0, 0.0)
    levels = []
    for size in (16, 32, 64):
        odd = (row // (2 * size) == lane // (2 * size)) & ((row // size) % 2 == 1)
        levels.append(jnp.where(odd & ((lane // size) % 2 == 0), 1.0, 0.0).astype(bf16))
    spread_from = [group16[:8] * 16 + r for r in range(15)]

    def one_head(g):
        if g in ARRIVE:
            for copy in fetch(ARRIVE.index(g)):
                copy.wait()
        cols = slice(g * 128, (g + 1) * 128)
        q = q_ref[:, cols]
        k, v = (ref[:, :, cols].reshape(STEPS, 128) for ref in (k_ref, v_ref))
        q32, k32, v32 = q.astype(f32), k.astype(f32), v.astype(f32)
        gram = dot_nt(k, k)
        scores = dot_nt(q, k)
        rk = lax.rsqrt(jnp.sum(k32 * k32, axis=1, keepdims=True) + epsilon)
        rq = lax.rsqrt(jnp.sum(q32 * q32, axis=1, keepdims=True) + epsilon)
        yield
        squares = [
            jnp.sum(jnp.where(eye, gram[a : a + 128, a : a + 128], 0.0), axis=0, keepdims=True)
            for a in (0, 128)
        ]
        rk_row = lax.rsqrt(across(*squares) + epsilon)
        c_row = cum[g : g + 1, :]
        c_col = columns[:, g : g + 1]
        b_col = columns[:, count_heads + g : count_heads + g + 1]
        be_col = columns[:, 2 * count_heads + g : 2 * count_heads + g + 1]
        f_col = columns[:, 3 * count_heads + g : 3 * count_heads + g + 1]
        ct_col = tok_columns[:, g : g + 1]
        et_col = tok_columns[:, count_heads + g : count_heads + g + 1]
        scale = b_col * rk

        def weighted(i, j):
            return (
                jnp.exp(c_col[i : i + 128] - c_row[:, j : j + 128])
                * gram[i : i + 128, j : j + 128]
                * scale[i : i + 128]
                * rk_row[:, j : j + 128]
            )

        lower = [jnp.where(strictly, weighted(a, a), 0.0) for a in (0, 128)]
        yield
        solved, compact = [eye16, eye16], []
        for part in lower:
            picked = part[:16]
            for b in range(1, 8):
                picked = jnp.where(group16 == b, part[16 * b : 16 * b + 16], picked)
            compact.append(picked)
        solved, compact = [[x[:8], x[8:]] for x in solved], [[x[:8], x[8:]] for x in compact]
        for r in range(15):
            for i in range(2):
                source = solved[i][r // 8][r % 8 : r % 8 + 1]
                for part in range((r + 1) // 8, 2):
                    spread = jnp.take_along_axis(compact[i][part], spread_from[r], axis=1)
                    solved[i][part] = solved[i][part] - spread * source
            if r % 5 == 4:
                yield
        one, two = [
            jnp.concatenate([jnp.where(group16 == b, down(*x), 0.0) for b in range(8)], axis=0)
            for x in solved
        ]
        low = [split(part) for part in lower]
        for odd in levels:
            picked = across(low[0][0] * odd, low[1][0] * odd)
            narrow = one.astype(bf16), two.astype(bf16)
            mid = dot(picked, paired(*narrow)).astype(bf16)
            yield
            out = dot(across(*narrow), paired(mid[:, :128], mid[:, 128:]))
            one, two = one - out[:, :128], two - out[:, 128:]
            yield
        rounded = one.astype(bf16), two.astype(bf16)
        pair = paired(*rounded)
        near = dot(across(low[0][0], low[1][0]), pair) + dot(across(low[0][1], low[1][1]), pair)
        rest = [
            (ones - part.astype(f32) - near[:, a : a + 128]).astype(bf16)
            for part, a in zip(rounded, (0, 128))
        ]
        yield
        out = dot(across(*rounded), paired(*rest)).astype(bf16)
        one, two = (rounded[0], out[:, :128]), (rounded[1], out[:, 128:])
        yield
        right = across((be_col * rk) * k32, b_col * v32)
        top = pieces_product(one, split(right[:128]))
        yield
        rest = right[128:] - pieces_product(split(weighted(128, 0)), split(top))
        yield
        bottom = pieces_product(two, split(rest))
        faded = (f_col * rk) * k32
        yield
        reads = jnp.where(visible, jnp.exp(ct_col - c_row) * scores * rq * rk_row, 0.0)
        x_high, x_low = split(down(top, bottom))
        p_high, p_low = split(down(across(faded[:128].T, faded[128:].T), reads))
        result = dot(p_high, x_high) + dot(p_low, x_high) + dot(p_high, x_low)
        yield
        lost = 1.0 - jnp.exp(end[g : g + 1])
        send_ref[g] = across(
            result[:128, :128] + jnp.where(eye, lost, 0.0), result[:128, 128:]
        ).astype(bf16)
        qe_ref[:, cols] = (et_col * rq) * q32 - result[128:, :128]
        lo_ref[:, cols] = result[128:, 128:]
        if g + 1 in LEAVE:
            for copy in put(LEAVE.index(g + 1) - 1):
                copy.start()

    waiting, running, tick = [one_head(g) for g in heads], [], 0
    while waiting or running:
        if waiting and tick % SKEW == 0:
            running.extend(waiting[:ABREAST])
            waiting = waiting[ABREAST:]
        running = [work for work in running if next(work, work) is None]
        tick += 1
    for batch in range(len(LEAVE) - 1):
        for copy in put(batch):
            copy.wait()


def local_part(query, keys, values, beta, gate_log, count):
    heads = gate_log.shape[0]
    anywhere = pl.BlockSpec(memory_space=pl.ANY)
    shapes = [((heads, 128, 256), bf16), (query.shape, f32), (query.shape, f32)]
    return pl.pallas_call(
        local_kernel,
        in_specs=[anywhere] * 3 + [pl.BlockSpec()] * 3,
        out_specs=[anywhere] * 3,
        out_shape=[jax.ShapeDtypeStruct(*shape) for shape in shapes],
        scratch_shapes=[
            *[pltpu.VMEM(x.shape, x.dtype) for x in (query, keys, values)],
            *[pltpu.VMEM(*shape) for shape in shapes],
            pltpu.SemaphoreType.DMA((3, len(ARRIVE) - 1)),
            pltpu.SemaphoreType.DMA((3, len(LEAVE) - 1)),
        ],
        name="local",
    )(query, keys, values, beta, gate_log, count)


def joined(later, earlier):
    f_high, f_low = split(later[:, :128])
    e_high, e_low = split(earlier)
    moved = dot(across(f_high, f_low), down(e_high, e_high)) + dot(f_high, e_low)
    return earlier + later - moved


def total_kernel(pieces_hbm, total_ref, mult_ref, add_ref, even_ref, pieces_ref, sems):
    chunks = pieces_hbm.shape[0]
    part = chunks // 2
    copies = [
        pltpu.make_async_copy(pieces_hbm.at[rows], pieces_ref.at[rows], sems.at[i])
        for i, rows in enumerate((pl.ds(0, part), pl.ds(part, part)))
    ]
    for copy in copies:
        copy.start()
    level, kept = [], []
    for c in range(0, chunks, 2):
        if c % part == 0:
            copies[c // part].wait()
        earlier, later = pieces_ref[c], pieces_ref[c + 1]
        even_ref[c // 2] = earlier
        level.append(earlier.astype(f32) + later.astype(f32) - dot(later[:, :128], earlier))
    kept = level[0::2]
    while len(level) > 1:
        level = [joined(level[i + 1], level[i]) for i in range(0, len(level), 2)]
        kept = level[0::2] + kept
    total_ref[...] = kept[0].astype(bf16)
    for i, node in enumerate(kept[1:]):
        mult_ref[i] = across(*split(node[:, :128]))
        add_ref[i] = node[:, 128:]


def states_kernel(
    plane_ref, one_ref, two_ref, three_ref, even_ref, mult_ref, add_ref, after_ref, out_ref
):
    plane = plane_ref[0]
    state = jnp.where(plane > 2, three_ref[:, 128:].astype(f32), 0.0)

    def stepped(piece, state):
        factor = piece[:, :128]
        high, low = split(state)
        moved = dot(across(factor, factor), down(high, low))
        return state + piece[:, 128:].astype(f32) - moved

    for back, ref in ((2, two_ref), (1, one_ref)):
        state = jnp.where(plane >= back, stepped(ref[...], state), 0.0)
    starts, node = [state], 0
    while len(starts) < even_ref.shape[0]:
        finer = []
        for state in starts:
            high, low = split(state)
            mult = mult_ref[node]
            moved = dot(mult, down(high, high)) + dot(mult[:, :128], low)
            finer += [state, state + add_ref[node] - moved]
            node += 1
        starts = finer
    for i, state in enumerate(starts):
        out_ref[2 * i] = state.astype(bf16)
        out_ref[2 * i + 1] = stepped(even_ref[i], state).astype(bf16)


def read_kernel(qe_ref, lo_ref, state_ref, gate_ref, gain_ref, out_ref):
    for g in range(state_ref.shape[0]):
        cols = slice(g * 128, (g + 1) * 128)
        high, low = split(qe_ref[:, cols])
        state = state_ref[g]
        out = lo_ref[:, cols] + dot(across(high, low), down(state, state))
        inverse_rms = lax.rsqrt(jnp.mean(out * out, axis=1, keepdims=True) + epsilon)
        gate = gate_ref[:, cols].astype(f32)
        silu = gate / (1.0 + jnp.exp(-gate))
        out_ref[:, cols] = (out * inverse_rms * gain_ref[...] * silu).astype(bf16)


def read_part(query_eff, local_out, states, out_gate, norm_gain):
    heads = states.shape[0]
    wide = GROUP * 128
    block = pl.BlockSpec((TOK, wide), lambda i: (0, i))
    return pl.pallas_call(
        read_kernel,
        grid=(heads // GROUP,),
        in_specs=[
            block,
            block,
            pl.BlockSpec((GROUP, 128, 128), lambda i: (i, 0, 0)),
            block,
            pl.BlockSpec((1, 128), lambda i: (0, 0)),
        ],
        out_specs=block,
        out_shape=jax.ShapeDtypeStruct(query_eff.shape, bf16),
        compiler_params=pltpu.CompilerParams(vmem_limit_bytes=32 * MIB),
        name="read",
    )(*map(in_hbm, (query_eff, local_out, states, out_gate, norm_gain.reshape(1, DV))))


def half_copy(half, weight_hbm, held_ref, sem):
    depth = held_ref.shape[0]
    rows = pl.ds(pl.multiple_of(half * depth, depth), depth)
    return pltpu.make_async_copy(weight_hbm.at[rows, :], held_ref, sem)


def hold_kernel(half_ref, after_hbm, weight_hbm, held_ref, sem):
    copy = half_copy(half_ref[0], weight_hbm, held_ref, sem)
    copy.start()
    copy.wait()


def own_kernel(half_ref, rows_ref, held_ref, weight_hbm, out_ref, other_ref, sem):
    copy = half_copy(1 - half_ref[0], weight_hbm, other_ref, sem)
    copy.start()
    out_ref[...] = dot(rows_ref[...], held_ref[...])
    copy.wait()


def other_kernel(rows_ref, held_ref, first_ref, out_ref):
    wide = out_ref.shape[1]
    for i in range(held_ref.shape[1] // wide):

        @pl.when(pl.program_id(0) == i)
        def _():
            part = held_ref[:, i * wide : (i + 1) * wide]
            out_ref[...] = (first_ref[...] + dot(rows_ref[...], part)).astype(bf16)


ANYWHERE = pl.BlockSpec(memory_space=pl.ANY)
SCALAR = pl.BlockSpec(memory_space=pltpu.SMEM)
ROOM = pltpu.CompilerParams(vmem_limit_bytes=32 * MIB)


def hold_half(half, after, weight):
    shape = (weight.shape[0] // 2, weight.shape[1])
    return pl.pallas_call(
        hold_kernel,
        in_specs=[SCALAR, ANYWHERE, ANYWHERE],
        out_specs=ANYWHERE,
        out_shape=jax.ShapeDtypeStruct(shape, bf16),
        scratch_shapes=[pltpu.SemaphoreType.DMA],
        compiler_params=ROOM,
        cost_estimate=pl.CostEstimate(flops=0, bytes_accessed=32 * MIB, transcendentals=0),
        name="hold",
    )(half, after, in_hbm(weight))


def own_half(half, rows, held, weight):
    return pl.pallas_call(
        own_kernel,
        in_specs=[SCALAR, pl.BlockSpec(), pl.BlockSpec(), ANYWHERE],
        out_specs=[pl.BlockSpec(), ANYWHERE],
        out_shape=[
            jax.ShapeDtypeStruct((TOK, weight.shape[1]), f32),
            jax.ShapeDtypeStruct(held.shape, bf16),
        ],
        scratch_shapes=[pltpu.SemaphoreType.DMA],
        compiler_params=ROOM,
        cost_estimate=pl.CostEstimate(
            flops=2 * TOK * held.size, bytes_accessed=2 * held.size, transcendentals=0
        ),
        name="own_half",
    )(half, rows, held, in_hbm(weight))


def other_half(rows, held, first):
    wide = held.shape[1] // 2
    block = pl.BlockSpec((TOK, wide), lambda i: (0, i))
    whole = pl.BlockSpec(memory_space=pltpu.VMEM)
    return pl.pallas_call(
        other_kernel,
        grid=(2,),
        in_specs=[whole, whole, block],
        out_specs=block,
        out_shape=jax.ShapeDtypeStruct(first.shape, bf16),
        compiler_params=ROOM,
        name="other_half",
    )(rows, held, first)


def shards(query, keys, values, beta, gate_log, house_count, out_gate, norm_gain, out_weight):
    heads = query.shape[1] // DK
    pieces, query_eff, local_out = local_part(
        query,
        keys,
        values,
        beta,
        gate_log,
        house_count.reshape(1, TOK),
    )
    mine = lax.all_to_all(pieces, PLANE, 0, 0, tiled=True)
    chunks = mine.shape[0]
    nodes = chunks // 2 - 1
    total, mult, add, even = pl.pallas_call(
        total_kernel,
        in_specs=[pl.BlockSpec(memory_space=pl.ANY)],
        out_shape=[
            jax.ShapeDtypeStruct((128, 256), bf16),
            jax.ShapeDtypeStruct((nodes, 128, 256), bf16),
            jax.ShapeDtypeStruct((nodes, 128, 128), f32),
            jax.ShapeDtypeStruct((chunks // 2, 128, 256), bf16),
        ],
        scratch_shapes=[pltpu.VMEM(mine.shape, bf16), pltpu.SemaphoreType.DMA((2,))],
        compiler_params=pltpu.CompilerParams(vmem_limit_bytes=32 * MIB),
        name="total",
    )(in_hbm(mine))
    planes = lax.axis_size("seq_0")
    before = [
        lax.ppermute(total, "seq_0", [(a, (a + s) % planes) for a in range(planes)])
        for s in range(planes - 1, 0, -1)
    ]
    half = lax.axis_index("head").reshape(1).astype(jnp.int32)
    held = hold_half(half, total, out_weight)
    plane = lax.axis_index("seq_0").reshape(1).astype(jnp.int32)
    states = pl.pallas_call(
        states_kernel,
        in_specs=[SCALAR] + [pl.BlockSpec()] * 6 + [ANYWHERE],
        out_shape=jax.ShapeDtypeStruct((chunks, 128, 128), bf16),
        compiler_params=pltpu.CompilerParams(vmem_limit_bytes=32 * MIB),
        name="states",
    )(plane, *before[::-1], even, mult, add, held)
    states = lax.all_to_all(states, PLANE, 0, 0, tiled=True)
    gated = read_part(query_eff, local_out, states, out_gate, norm_gain)
    other = lax.ppermute(gated, "head", [(0, 1), (1, 0)])
    partial, rest = own_half(half, gated, held, out_weight)
    return other_half(other, rest, partial)


def solution(mesh):
    finer = Mesh(
        mesh.devices.reshape(4, 4, 4, mesh.shape["head"]), ("seq_0", "seq_1", "seq_2", "head")
    )
    in_specs = (
        P(SEQ, "head"),
        P(SEQ, None, "head"),
        P(SEQ, None, "head"),
        P(None, "head", SEQ),
        P("head", SEQ),
        P(SEQ),
        P(SEQ, "head"),
        P(),
        P(None, "head"),
    )
    out_specs = P(SEQ, "head")
    return jax.shard_map(
        shards, mesh=finer, in_specs=in_specs, out_specs=out_specs, check_vma=False
    )
```

```python
import functools

import jax
import jax.numpy as jnp
from jax import lax
from jax.experimental import pallas as pl
from jax.experimental.pallas import tpu as pltpu
from jax.sharding import Mesh
from jax.sharding import PartitionSpec as P

DK = 128
DV = 128
NH = 2
TOK = 128
STEPS = TOK * NH
SEQ = ("seq_0", "seq_1", "seq_2")
PLANE = ("seq_1", "seq_2")
GROUP = 8
ARRIVE = (0, 4, 16)
LEAVE = (0, 8, 13, 16)
SKEW = 1
ABREAST = 1
MIB = 1024 * 1024
epsilon = 1e-06
f32, bf16 = jnp.float32, jnp.bfloat16


def dot(a, b):
    return jnp.dot(a, b, preferred_element_type=f32)


def dot_nt(a, b):
    return lax.dot_general(a, b, (((1,), (1,)), ((), ())), preferred_element_type=f32)


def split(x):
    high = x.astype(bf16)
    return high, (x - high.astype(f32)).astype(bf16)


def across(a, b):
    return jnp.concatenate([a, b], axis=1)


def down(a, b):
    return jnp.concatenate([a, b], axis=0)


def paired(a, b):
    zero = jnp.zeros_like(a)
    return down(across(a, zero), across(zero, b))


def pieces_product(a, b):
    (a_high, a_low), (b_high, b_low) = a, b
    return dot(across(a_high, a_low), down(b_high, b_high)) + dot(a_high, b_low)


def in_hbm(x):
    return pltpu.with_memory_space_constraint(x, pltpu.HBM)


def iota(shape, dim):
    return lax.broadcasted_iota(jnp.int32, shape, dim)


def local_kernel(
    q_hbm, k_hbm, v_hbm, beta_ref, gate_ref, count_ref, send_hbm, qe_hbm, lo_hbm,
    q_ref, k_ref, v_ref, send_ref, qe_ref, lo_ref, in_sems, out_sems,
):
    count_heads = gate_ref.shape[0]
    heads = range(count_heads)

    def fetch(batch):
        first, last = ARRIVE[batch], ARRIVE[batch + 1]
        cols = pl.ds(first * 128, (last - first) * 128)
        return [
            pltpu.make_async_copy(k_hbm.at[:, :, cols], k_ref.at[:, :, cols], in_sems.at[0, batch]),
            pltpu.make_async_copy(v_hbm.at[:, :, cols], v_ref.at[:, :, cols], in_sems.at[1, batch]),
            pltpu.make_async_copy(q_hbm.at[:, cols], q_ref.at[:, cols], in_sems.at[2, batch]),
        ]

    def put(batch):
        first, last = LEAVE[batch], LEAVE[batch + 1]
        rows, cols = pl.ds(first, last - first), pl.ds(first * 128, (last - first) * 128)
        return [
            pltpu.make_async_copy(send_ref.at[rows], send_hbm.at[rows], out_sems.at[0, batch]),
            pltpu.make_async_copy(qe_ref.at[:, cols], qe_hbm.at[:, cols], out_sems.at[1, batch]),
            pltpu.make_async_copy(lo_ref.at[:, cols], lo_hbm.at[:, cols], out_sems.at[2, batch]),
        ]

    for batch in range(len(ARRIVE) - 1):
        for copy in fetch(batch):
            copy.start()
    token, step = iota((TOK, STEPS), 0), iota((TOK, STEPS), 1)
    highest = lax.Precision.HIGHEST

    def place(rows, chosen):
        return jnp.dot(rows, chosen.astype(f32), precision=highest, preferred_element_type=f32)

    gates = gate_ref[...]
    count = count_ref[...]
    cum = place(gates, token * NH <= step)
    cum_tok = place(gates, iota((TOK, TOK), 0) <= iota((TOK, TOK), 1))
    strength = sum(
        place(jnp.where(j < count, beta_ref[j], 0.0), step == token * NH + j)
        for j in range(NH)
    )
    end = cum[:, STEPS - 1 :]
    stacked = jnp.concatenate(
        [
            cum,
            strength,
            strength * jnp.exp(cum),
            jnp.exp(end - cum),
            jnp.zeros((128 - 4 * count_heads, STEPS), f32),
        ],
        axis=0,
    )
    columns = down(stacked[:, :128].T, stacked[:, 128:].T)
    tok_columns = jnp.concatenate(
        [cum_tok, jnp.exp(cum_tok), jnp.zeros((128 - 2 * count_heads, TOK), f32)], axis=0
    ).T

    row, lane = iota((128, 128), 0), iota((128, 128), 1)
    eye = row == lane
    strictly = row > lane
    lane16 = iota((16, 128), 1)
    group16 = lane16 // 16
    eye16 = jnp.where(iota((16, 128), 0) == lane16 % 16, 1.0, 0.0).astype(f32)
    visible = step <= token * NH + (NH - 1)

    ones = jnp.where(eye, 1.0, 0.0)
    levels = []
    for size in (16, 32, 64):
        odd = (row // (2 * size) == lane // (2 * size)) & ((row // size) % 2 == 1)
        levels.append(jnp.where(odd & ((lane // size) % 2 == 0), 1.0, 0.0).astype(bf16))
    spread_from = [group16[:8] * 16 + r for r in range(15)]

    def one_head(g):
        if g in ARRIVE:
            for copy in fetch(ARRIVE.index(g)):
                copy.wait()
        cols = slice(g * 128, (g + 1) * 128)
        q = q_ref[:, cols]
        k, v = (ref[:, :, cols].reshape(STEPS, 128) for ref in (k_ref, v_ref))
        q32, k32, v32 = q.astype(f32), k.astype(f32), v.astype(f32)
        gram = dot_nt(k, k)
        scores = dot_nt(q, k)
        rk = lax.rsqrt(jnp.sum(k32 * k32, axis=1, keepdims=True) + epsilon)
        rq = lax.rsqrt(jnp.sum(q32 * q32, axis=1, keepdims=True) + epsilon)
        yield
        squares = [
            jnp.sum(jnp.where(eye, gram[a : a + 128, a : a + 128], 0.0), axis=0, keepdims=True)
            for a in (0, 128)
        ]
        rk_row = lax.rsqrt(across(*squares) + epsilon)
        c_row = cum[g : g + 1, :]
        c_col = columns[:, g : g + 1]
        b_col = columns[:, count_heads + g : count_heads + g + 1]
        be_col = columns[:, 2 * count_heads + g : 2 * count_heads + g + 1]
        f_col = columns[:, 3 * count_heads + g : 3 * count_heads + g + 1]
        ct_col = tok_columns[:, g : g + 1]
        et_col = tok_columns[:, count_heads + g : count_heads + g + 1]
        scale = b_col * rk

        def weighted(i, j):
            return (
                jnp.exp(c_col[i : i + 128] - c_row[:, j : j + 128])
                * gram[i : i + 128, j : j + 128]
                * scale[i : i + 128]
                * rk_row[:, j : j + 128]
            )

        lower = [jnp.where(strictly, weighted(a, a), 0.0) for a in (0, 128)]
        yield
        solved, compact = [eye16, eye16], []
        for part in lower:
            picked = part[:16]
            for b in range(1, 8):
                picked = jnp.where(group16 == b, part[16 * b : 16 * b + 16], picked)
            compact.append(picked)
        solved, compact = [[x[:8], x[8:]] for x in solved], [[x[:8], x[8:]] for x in compact]
        for r in range(15):
            for i in range(2):
                source = solved[i][r // 8][r % 8 : r % 8 + 1]
                for part in range((r + 1) // 8, 2):
                    spread = jnp.take_along_axis(compact[i][part], spread_from[r], axis=1)
                    solved[i][part] = solved[i][part] - spread * source
            if r % 5 == 4:
                yield
        one, two = [
            jnp.concatenate([jnp.where(group16 == b, down(*x), 0.0) for b in range(8)], axis=0)
            for x in solved
        ]
        low = [split(part) for part in lower]
        for odd in levels:
            picked = across(low[0][0] * odd, low[1][0] * odd)
            narrow = one.astype(bf16), two.astype(bf16)
            mid = dot(picked, paired(*narrow)).astype(bf16)
            yield
            out = dot(across(*narrow), paired(mid[:, :128], mid[:, 128:]))
            one, two = one - out[:, :128], two - out[:, 128:]
            yield
        rounded = one.astype(bf16), two.astype(bf16)
        pair = paired(*rounded)
        near = dot(across(low[0][0], low[1][0]), pair) + dot(across(low[0][1], low[1][1]), pair)
        rest = [
            (ones - part.astype(f32) - near[:, a : a + 128]).astype(bf16)
            for part, a in zip(rounded, (0, 128))
        ]
        yield
        out = dot(across(*rounded), paired(*rest)).astype(bf16)
        one, two = (rounded[0], out[:, :128]), (rounded[1], out[:, 128:])
        yield
        right = across((be_col * rk) * k32, b_col * v32)
        top = pieces_product(one, split(right[:128]))
        yield
        rest = right[128:] - pieces_product(split(weighted(128, 0)), split(top))
        yield
        bottom = pieces_product(two, split(rest))
        faded = (f_col * rk) * k32
        yield
        reads = jnp.where(visible, jnp.exp(ct_col - c_row) * scores * rq * rk_row, 0.0)
        x_high, x_low = split(down(top, bottom))
        p_high, p_low = split(down(across(faded[:128].T, faded[128:].T), reads))
        result = dot(p_high, x_high) + dot(p_low, x_high) + dot(p_high, x_low)
        yield
        lost = 1.0 - jnp.exp(end[g : g + 1])
        send_ref[g] = across(
            result[:128, :128] + jnp.where(eye, lost, 0.0), result[:128, 128:]
        ).astype(bf16)
        qe_ref[:, cols] = (et_col * rq) * q32 - result[128:, :128]
        lo_ref[:, cols] = result[128:, 128:]
        if g + 1 in LEAVE:
            for copy in put(LEAVE.index(g + 1) - 1):
                copy.start()

    waiting, running, tick = [one_head(g) for g in heads], [], 0
    while waiting or running:
        if waiting and tick % SKEW == 0:
            running.extend(waiting[:ABREAST])
            waiting = waiting[ABREAST:]
        running = [work for work in running if next(work, work) is None]
        tick += 1
    for batch in range(len(LEAVE) - 1):
        for copy in put(batch):
            copy.wait()


def local_part(query, keys, values, beta, gate_log, count):
    heads = gate_log.shape[0]
    anywhere = pl.BlockSpec(memory_space=pl.ANY)
    shapes = [((heads, 128, 256), bf16), (query.shape, f32), (query.shape, f32)]
    return pl.pallas_call(
        local_kernel,
        in_specs=[anywhere] * 3 + [pl.BlockSpec()] * 3,
        out_specs=[anywhere] * 3,
        out_shape=[jax.ShapeDtypeStruct(*shape) for shape in shapes],
        scratch_shapes=[
            *[pltpu.VMEM(x.shape, x.dtype) for x in (query, keys, values)],
            *[pltpu.VMEM(*shape) for shape in shapes],
            pltpu.SemaphoreType.DMA((3, len(ARRIVE) - 1)),
            pltpu.SemaphoreType.DMA((3, len(LEAVE) - 1)),
        ],
        compiler_params=pltpu.CompilerParams(vmem_limit_bytes=40 * MIB),
        name="local",
    )(*map(in_hbm, (query, keys, values, beta, gate_log, count)))


def joined(later, earlier):
    f_high, f_low = split(later[:, :128])
    e_high, e_low = split(earlier)
    moved = dot(across(f_high, f_low), down(e_high, e_high)) + dot(f_high, e_low)
    return earlier + later - moved


def total_kernel(pieces_hbm, total_ref, mult_ref, add_ref, even_ref, pieces_ref, sems):
    chunks = pieces_hbm.shape[0]
    part = chunks // 2
    copies = [
        pltpu.make_async_copy(pieces_hbm.at[rows], pieces_ref.at[rows], sems.at[i])
        for i, rows in enumerate((pl.ds(0, part), pl.ds(part, part)))
    ]
    for copy in copies:
        copy.start()
    level, kept = [], []
    for c in range(0, chunks, 2):
        if c % part == 0:
            copies[c // part].wait()
        earlier, later = pieces_ref[c], pieces_ref[c + 1]
        even_ref[c // 2] = earlier
        level.append(earlier.astype(f32) + later.astype(f32) - dot(later[:, :128], earlier))
    kept = level[0::2]
    while len(level) > 1:
        level = [joined(level[i + 1], level[i]) for i in range(0, len(level), 2)]
        kept = level[0::2] + kept
    total_ref[...] = kept[0].astype(bf16)
    for i, node in enumerate(kept[1:]):
        mult_ref[i] = across(*split(node[:, :128]))
        add_ref[i] = node[:, 128:]


def states_kernel(
    plane_ref, one_ref, two_ref, three_ref, even_ref, mult_ref, add_ref, after_ref, out_ref
):
    plane = plane_ref[0]
    state = jnp.where(plane > 2, three_ref[:, 128:].astype(f32), 0.0)

    def stepped(piece, state):
        factor = piece[:, :128]
        high, low = split(state)
        moved = dot(across(factor, factor), down(high, low))
        return state + piece[:, 128:].astype(f32) - moved

    for back, ref in ((2, two_ref), (1, one_ref)):
        state = jnp.where(plane >= back, stepped(ref[...], state), 0.0)
    starts, node = [state], 0
    while len(starts) < even_ref.shape[0]:
        finer = []
        for state in starts:
            high, low = split(state)
            mult = mult_ref[node]
            moved = dot(mult, down(high, high)) + dot(mult[:, :128], low)
            finer += [state, state + add_ref[node] - moved]
            node += 1
        starts = finer
    for i, state in enumerate(starts):
        out_ref[2 * i] = state.astype(bf16)
        out_ref[2 * i + 1] = stepped(even_ref[i], state).astype(bf16)


def read_kernel(qe_ref, lo_ref, state_ref, gate_ref, gain_ref, out_ref):
    for g in range(state_ref.shape[0]):
        cols = slice(g * 128, (g + 1) * 128)
        high, low = split(qe_ref[:, cols])
        state = state_ref[g]
        out = lo_ref[:, cols] + dot(across(high, low), down(state, state))
        inverse_rms = lax.rsqrt(jnp.mean(out * out, axis=1, keepdims=True) + epsilon)
        gate = gate_ref[:, cols].astype(f32)
        silu = gate / (1.0 + jnp.exp(-gate))
        out_ref[:, cols] = (out * inverse_rms * gain_ref[...] * silu).astype(bf16)


def read_part(query_eff, local_out, states, out_gate, norm_gain):
    heads = states.shape[0]
    wide = GROUP * 128
    block = pl.BlockSpec((TOK, wide), lambda i: (0, i))
    return pl.pallas_call(
        read_kernel,
        grid=(heads // GROUP,),
        in_specs=[
            block,
            block,
            pl.BlockSpec((GROUP, 128, 128), lambda i: (i, 0, 0)),
            block,
            pl.BlockSpec((1, 128), lambda i: (0, 0)),
        ],
        out_specs=block,
        out_shape=jax.ShapeDtypeStruct(query_eff.shape, bf16),
        compiler_params=pltpu.CompilerParams(vmem_limit_bytes=32 * MIB),
        name="read",
    )(query_eff, local_out, *map(in_hbm, (states, out_gate, norm_gain.reshape(1, DV))))


def half_copy(half, weight_hbm, held_ref, sem):
    depth = held_ref.shape[0]
    rows = pl.ds(pl.multiple_of(half * depth, depth), depth)
    return pltpu.make_async_copy(weight_hbm.at[rows, :], held_ref, sem)


def hold_kernel(half_ref, after_hbm, weight_hbm, held_ref, sem):
    copy = half_copy(half_ref[0], weight_hbm, held_ref, sem)
    copy.start()
    copy.wait()


def own_kernel(half_ref, rows_ref, held_ref, weight_hbm, out_ref, other_ref, sem):
    copy = half_copy(1 - half_ref[0], weight_hbm, other_ref, sem)
    copy.start()
    out_ref[...] = dot(rows_ref[...], held_ref[...])
    copy.wait()


def other_kernel(rows_ref, held_ref, first_ref, out_ref):
    wide = out_ref.shape[1]
    for i in range(held_ref.shape[1] // wide):

        @pl.when(pl.program_id(0) == i)
        def _():
            part = held_ref[:, i * wide : (i + 1) * wide]
            out_ref[...] = (first_ref[...] + dot(rows_ref[...], part)).astype(bf16)


ANYWHERE = pl.BlockSpec(memory_space=pl.ANY)
SCALAR = pl.BlockSpec(memory_space=pltpu.SMEM)
ROOM = pltpu.CompilerParams(vmem_limit_bytes=32 * MIB)


def hold_half(half, after, weight):
    shape = (weight.shape[0] // 2, weight.shape[1])
    return pl.pallas_call(
        hold_kernel,
        in_specs=[SCALAR, ANYWHERE, ANYWHERE],
        out_specs=ANYWHERE,
        out_shape=jax.ShapeDtypeStruct(shape, bf16),
        scratch_shapes=[pltpu.SemaphoreType.DMA],
        compiler_params=ROOM,
        cost_estimate=pl.CostEstimate(flops=0, bytes_accessed=32 * MIB, transcendentals=0),
        name="hold",
    )(half, after, in_hbm(weight))


def own_half(half, rows, held, weight):
    return pl.pallas_call(
        own_kernel,
        in_specs=[SCALAR, pl.BlockSpec(), pl.BlockSpec(), ANYWHERE],
        out_specs=[pl.BlockSpec(), ANYWHERE],
        out_shape=[
            jax.ShapeDtypeStruct((TOK, weight.shape[1]), f32),
            jax.ShapeDtypeStruct(held.shape, bf16),
        ],
        scratch_shapes=[pltpu.SemaphoreType.DMA],
        compiler_params=ROOM,
        cost_estimate=pl.CostEstimate(
            flops=2 * TOK * held.size, bytes_accessed=2 * held.size, transcendentals=0
        ),
        name="own_half",
    )(half, rows, held, in_hbm(weight))


def other_half(rows, held, first):
    wide = held.shape[1] // 2
    block = pl.BlockSpec((TOK, wide), lambda i: (0, i))
    whole = pl.BlockSpec(memory_space=pltpu.VMEM)
    return pl.pallas_call(
        other_kernel,
        grid=(2,),
        in_specs=[whole, whole, block],
        out_specs=block,
        out_shape=jax.ShapeDtypeStruct(first.shape, bf16),
        compiler_params=ROOM,
        name="other_half",
    )(rows, held, first)


def shards(query, keys, values, beta, gate_log, house_count, out_gate, norm_gain, out_weight):
    heads = query.shape[1] // DK
    pieces, query_eff, local_out = local_part(
        query,
        keys,
        values,
        beta,
        gate_log,
        house_count.reshape(1, TOK),
    )
    mine = lax.all_to_all(pieces, PLANE, 0, 0, tiled=True)
    chunks = mine.shape[0]
    nodes = chunks // 2 - 1
    total, mult, add, even = pl.pallas_call(
        total_kernel,
        in_specs=[pl.BlockSpec(memory_space=pl.ANY)],
        out_shape=[
            jax.ShapeDtypeStruct((128, 256), bf16),
            jax.ShapeDtypeStruct((nodes, 128, 256), bf16),
            jax.ShapeDtypeStruct((nodes, 128, 128), f32),
            jax.ShapeDtypeStruct((chunks // 2, 128, 256), bf16),
        ],
        scratch_shapes=[pltpu.VMEM(mine.shape, bf16), pltpu.SemaphoreType.DMA((2,))],
        compiler_params=pltpu.CompilerParams(vmem_limit_bytes=32 * MIB),
        name="total",
    )(in_hbm(mine))
    planes = lax.axis_size("seq_0")
    before = [
        lax.ppermute(total, "seq_0", [(a, (a + s) % planes) for a in range(planes)])
        for s in range(planes - 1, 0, -1)
    ]
    half = lax.axis_index("head").reshape(1).astype(jnp.int32)
    held = hold_half(half, total, out_weight)
    plane = lax.axis_index("seq_0").reshape(1).astype(jnp.int32)
    states = pl.pallas_call(
        states_kernel,
        in_specs=[SCALAR] + [pl.BlockSpec()] * 6 + [ANYWHERE],
        out_shape=jax.ShapeDtypeStruct((chunks, 128, 128), bf16),
        compiler_params=pltpu.CompilerParams(vmem_limit_bytes=32 * MIB),
        name="states",
    )(plane, *before[::-1], even, mult, add, held)
    states = lax.all_to_all(states, PLANE, 0, 0, tiled=True)
    gated = read_part(query_eff, local_out, states, out_gate, norm_gain)
    other = lax.ppermute(gated, "head", [(0, 1), (1, 0)])
    partial, rest = own_half(half, gated, held, out_weight)
    return other_half(other, rest, partial)


def solution(mesh):
    finer = Mesh(
        mesh.devices.reshape(4, 4, 4, mesh.shape["head"]), ("seq_0", "seq_1", "seq_2", "head")
    )
    in_specs = (
        P(SEQ, "head"),
        P(SEQ, None, "head"),
        P(SEQ, None, "head"),
        P(None, "head", SEQ),
        P("head", SEQ),
        P(SEQ),
        P(SEQ, "head"),
        P(),
        P(None, "head"),
    )
    out_specs = P(SEQ, "head")
    return jax.shard_map(
        shards, mesh=finer, in_specs=in_specs, out_specs=out_specs, check_vma=False
    )
```
